32 devices in a mesh: dp: 2 (over x), ctx: 16 (over z, y, core).
Axes of the slice: x: 2, y: 2, z: 4, core: 2. Of those that a mesh axis runs over, the one named last changes fastest.
Arguments:
- query_rows: bfloat16 [2, 4096, 2048], P('dp', 'ctx')
- key_rows: bfloat16 [2, 4096, 512], P('dp', 'ctx')
- value_rows: bfloat16 [2, 4096, 512], P('dp', 'ctx'), may hold values from -6 to 6
- out_grad: bfloat16 [2, 4096, 2048], P('dp', 'ctx'), may hold values from -6 to 6
- lengths: int32 [2, 8], P('dp'), may hold values from 1 to 1024, 4096 in all within a row
- loss_mask: int32 [2, 4096], P('dp', 'ctx'), may hold values from 0 to 1
Outputs:
- query_grad: bfloat16 [2, 4096, 2048], P('dp', 'ctx')
- key_grad: bfloat16 [2, 4096, 512], P('dp', 'ctx')
- value_grad: bfloat16 [2, 4096, 512], P('dp', 'ctx')
The draws below stay inside these ranges and needn't reach their ends.
Inputs may be any that keep to these rules, and one draw needn't show every extreme that they name: `lengths`: each row sums to 4096, and its largest entry is exactly 1024.
All inputs are finite; a program needn't handle non-finite values.
Results may differ from the reference program's by a relative error of at most 0.017.
Values may be sent and summed in bfloat16 or wider, within the bound.
No kernel may reach another device: no remote copies, remote signals or barrier semaphores. Data moves between devices by JAX's collectives and lax.ppermute only.
A program may use at most 64 MiB of HBM per device.

```python
import math
import jax
import jax.numpy as jnp
import numpy as np
from jax import lax

HQ = 16
HK = 4
HD = 128
TOK_DEV = 256
WIN = 4
B = 2
SEQ = 4096
DOC_MOST = 1024
NDOCS = 8


def draw_query_rows(key, part):
    base_key = jax.random.fold_in(key, 5)
    values_out = jnp.clip(jax.random.normal(base_key, (B, SEQ, HQ * HD), jnp.float32), -6.0, 6.0)
    return values_out.astype(jnp.bfloat16)


def draw_key_rows(key, part):
    base_key = jax.random.fold_in(key, 6)
    values_out = jnp.clip(jax.random.normal(base_key, (B, SEQ, HK * HD), jnp.float32), -6.0, 6.0)
    return values_out.astype(jnp.bfloat16)


def draw_loss_mask(key, part):
    base_level = jax.random.randint(jax.random.fold_in(key, 21), (B, 1), 200, 300)
    places = jnp.arange(SEQ, dtype=jnp.int32)[None, :]
    threshold = base_level * (SEQ + 2 * places) // SEQ
    uniform_ints = jax.random.randint(jax.random.fold_in(key, 22), (B, SEQ), 0, 1000)
    return (uniform_ints < threshold).astype(jnp.int32)


def shard_levels(own_key, shape, pieces, smallest, high):
    loudness = 1.0
    for position, blocks in pieces:
        draws = jax.random.uniform(jax.random.fold_in(jax.random.fold_in(own_key, 6), position), (blocks,), jnp.float32, smallest / len(pieces), high / len(pieces))
        loudness = loudness * jnp.repeat(jnp.exp(draws), shape[position] // blocks).reshape((-1,) + (1,) * (len(shape) - 1 - position))
    return loudness


def length_profile(count, total, bound, lean):
    loads = [(1 << 20) // math.isqrt(grade ** lean) + 1 for grade in range(2, count + 1)]
    surplus, holding = total - bound - (count - 1), [1] * (count - 1)
    while surplus > 0:
        candidates = [i for i in range(count - 1) if holding[i] < bound]
        whole, left = sum([loads[i] for i in candidates]), surplus
        for i in candidates:
            more = min(bound - holding[i], max(1, left * loads[i] // whole), surplus)
            holding[i] = holding[i] + more
            surplus = surplus - more
    return np.array([bound] + holding)


def ragged(key, count, total, most, slope):
    if count == 2:
        one = jax.random.randint(key, (), max(1, total - most), min(most, total - 1) + 1)
        return jnp.stack([one, total - one])
    sizes = jnp.asarray(length_profile(count, total, most, slope), jnp.int32)
    pairs = (count - 1) // 2
    source_of, taker = sizes[1:1 + 2 * pairs:2], sizes[2:2 + 2 * pairs:2]
    slack = jnp.minimum(source_of - 1, most - taker)
    moved = jax.random.randint(jax.random.fold_in(key, 1), (pairs,), 0, 1 << 20) % (slack + 1)
    sizes = sizes.at[1:1 + 2 * pairs:2].set(source_of - moved).at[2:2 + 2 * pairs:2].set(taker + moved)
    return sizes[jax.random.permutation(jax.random.fold_in(key, 2), count)]


def scatter_about(rng, dims, deviation, bound, cuts=(), held_as=jnp.bfloat16):
    loudness = shard_levels(rng, dims, cuts, -0.22, 0.18) if cuts else 1.0
    entries = jax.random.normal(rng, dims, jnp.float32) * deviation * loudness
    return jnp.minimum(jnp.maximum(entries, -bound), bound).astype(held_as)


def setup_inputs(seed: int = 0) -> dict:
    keys = jax.random.split(jax.random.key(seed), 7)
    return {
        "query_rows": draw_query_rows(jax.random.fold_in(keys[6], 71), 0),
        "key_rows": draw_key_rows(jax.random.fold_in(keys[6], 71), 0),
        "value_rows": scatter_about(keys[2], (B, SEQ, HK * HD), 1.0, 6.0, ((0, 2), (1, 16))),
        "out_grad": scatter_about(keys[3], (B, SEQ, HQ * HD), 1.0, 6.0, ((0, 2), (1, 16))),
        "lengths": jax.vmap(lambda own: ragged(own, NDOCS, SEQ, DOC_MOST, 2))(jax.random.split(keys[4], B)).reshape((B, NDOCS)).astype(jnp.int32),
        "loss_mask": draw_loss_mask(jax.random.fold_in(keys[6], 71), 0),
    }


def doc_index(bounds, where):
    return jnp.sum((bounds[None, :] <= where[:, None]).astype(jnp.int32), axis=1)


def reference(query_rows, key_rows, value_rows, out_grad, lengths, loss_mask):
    group_size = HQ // HK
    scale = HD ** -0.5
    reach = WIN * TOK_DEV
    key_span = (WIN + 1) * TOK_DEV
    hip = lax.Precision.HIGHEST
    token_total = jnp.sum(loss_mask.astype(jnp.float32))
    loss_scale = (B * SEQ) / token_total
    grads_in = (out_grad.astype(jnp.float32) * loss_mask[:, :, None].astype(jnp.float32) * loss_scale).astype(jnp.bfloat16)
    query_list = []
    key_list = []
    value_list = []
    for seq_index in range(B):
        bounds = jnp.cumsum(lengths[seq_index]).astype(jnp.int32)
        positions = jnp.arange(SEQ, dtype=jnp.int32)
        doc_ids = doc_index(bounds, positions)
        pad_docs = jnp.concatenate([jnp.full((reach,), -1, jnp.int32), doc_ids])
        pad_pos = jnp.arange(SEQ + reach, dtype=jnp.int32) - reach
        pad_keys = jnp.concatenate([jnp.zeros((reach, HK * HD), jnp.float32), key_rows[seq_index].astype(jnp.float32)])
        pad_values = jnp.concatenate([jnp.zeros((reach, HK * HD), jnp.float32), value_rows[seq_index].astype(jnp.float32)])
        queries = query_rows[seq_index].astype(jnp.float32)
        grad_rows = grads_in[seq_index].astype(jnp.float32)

        def block_step(state_in, block_index):
            key_acc, value_acc = state_in
            start = (block_index * TOK_DEV).astype(jnp.int32)
            query_block = lax.dynamic_slice_in_dim(queries, start, TOK_DEV, 0).reshape(TOK_DEV, HK, group_size, HD)
            grad_block = lax.dynamic_slice_in_dim(grad_rows, start, TOK_DEV, 0).reshape(TOK_DEV, HK, group_size, HD)
            query_pos = lax.dynamic_slice_in_dim(positions, start, TOK_DEV, 0)
            query_docs = lax.dynamic_slice_in_dim(doc_ids, start, TOK_DEV, 0)
            key_block = lax.dynamic_slice_in_dim(pad_keys, start, key_span, 0).reshape(key_span, HK, HD)
            value_block = lax.dynamic_slice_in_dim(pad_values, start, key_span, 0).reshape(key_span, HK, HD)
            key_pos = lax.dynamic_slice_in_dim(pad_pos, start, key_span, 0)
            key_docs = lax.dynamic_slice_in_dim(pad_docs, start, key_span, 0)
            allowed = (query_docs[:, None] == key_docs[None, :]) & (key_pos[None, :] <= query_pos[:, None])
            scores = jnp.einsum("rkgd,ckd->kgrc", query_block, key_block, precision=hip) * scale
            scores = jnp.where(allowed[None, None], scores, -jnp.inf)
            log_mass = jax.nn.logsumexp(scores, axis=-1)
            weights = jnp.exp(scores - log_mass[..., None])
            probs = lax.optimization_barrier(weights.astype(jnp.bfloat16)).astype(jnp.float32)
            attended = jnp.einsum("kgrc,ckd->rkgd", probs, value_block, precision=hip)
            grad_dot = jnp.einsum("rkgd,rkgd->kgr", grad_block, attended, precision=hip)
            dprobs = jnp.einsum("rkgd,ckd->kgrc", grad_block, value_block, precision=hip)
            dscores = (weights * (dprobs - grad_dot[..., None]) * scale).astype(jnp.bfloat16)
            dscores = lax.optimization_barrier(dscores).astype(jnp.float32)
            query_part = jnp.einsum("kgrc,ckd->rkgd", dscores, key_block, precision=hip).reshape(TOK_DEV, HQ * HD)
            key_part = jnp.einsum("kgrc,rkgd->ckd", dscores, query_block, precision=hip).reshape(key_span, HK * HD)
            value_part = jnp.einsum("kgrc,rkgd->ckd", probs, grad_block, precision=hip).reshape(key_span, HK * HD)
            key_acc = lax.dynamic_update_slice_in_dim(key_acc, lax.dynamic_slice_in_dim(key_acc, start, key_span, 0) + key_part, start, 0)
            value_acc = lax.dynamic_update_slice_in_dim(value_acc, lax.dynamic_slice_in_dim(value_acc, start, key_span, 0) + value_part, start, 0)
            return (key_acc, value_acc), query_part.astype(jnp.bfloat16)

        empty = jnp.zeros((SEQ + reach, HK * HD), jnp.float32)
        (key_acc, value_acc), query_parts = lax.scan(block_step, (empty, empty), jnp.arange(SEQ // TOK_DEV, dtype=jnp.int32))
        query_list.append(query_parts.reshape(SEQ, HQ * HD))
        key_list.append(key_acc[reach:].astype(jnp.bfloat16))
        value_list.append(value_acc[reach:].astype(jnp.bfloat16))
    return (jnp.stack(query_list), jnp.stack(key_list), jnp.stack(value_list))
```

```python
import math

import jax
import jax.numpy as jnp
from jax import lax
from jax.experimental import pallas as pl
from jax.experimental.pallas import tpu as pltpu
from jax.sharding import PartitionSpec as P

HQ = 16
HK = 4
HD = 128
WIN = 4
GROUP = HQ // HK
MINE = HK // 2
BLOCKS = WIN + 2
EXP2_SCALE = HD ** (-0.5) * math.log2(math.e)


def shifted(value, by):
    count = lax.axis_size("ctx")
    pairs = [(i, i + by) for i in range(count) if 0 <= i + by < count]
    return lax.ppermute(value, "ctx", pairs)


def swapped(value, bit):
    count = lax.axis_size("ctx")
    return lax.ppermute(value, "ctx", [(i, i ^ bit) for i in range(count)])


def everywhere_sum(value):
    dp_count = lax.axis_size("dp")
    step = 1
    while step < dp_count:
        value = value + lax.ppermute(value, "dp", [(i, i ^ step) for i in range(dp_count)])
        step *= 2
    step = 1
    while step < lax.axis_size("ctx"):
        value = value + swapped(value, step)
        step *= 2
    return value


def nt(a, b):
    return lax.dot_general(a, b, (((1,), (1,)), ((), ())), preferred_element_type=jnp.float32)


def nn(a, b):
    return lax.dot_general(a, b, (((1,), (0,)), ((), ())), preferred_element_type=jnp.float32)


def grads_kernel(
    lengths_ref, where_ref, own_q, sib_q, own_g, sib_g, kv0, kv1, kv2,
    own_dq, sib_dq, out0, out1, out2,
    q_s, g_s, k_s, v_s, kt_s, e_s, dp_s, mb_s, m_s, l_s, w_s, dqt_s, dk_s, dv_s,
):
    rows = own_q.shape[0]
    my_index = where_ref[0]
    doc_count = lengths_ref.shape[1]
    for h in range(GROUP):
        columns = slice(h * HD, (h + 1) * HD)
        q_s[h] = own_q[:, columns]
        q_s[GROUP + h] = sib_q[:, columns]
        g_s[h] = own_g[:, columns]
        g_s[GROUP + h] = sib_g[:, columns]
    for d, kv in enumerate((kv0, kv1, kv2)):
        for p in range(2):
            k_s[2 * d + p] = kv[0, p]
            v_s[2 * d + p] = kv[1, p]
            kt_s[2 * d + p] = kv[0, p].T
    dk_s[...] = jnp.zeros_like(dk_s)
    dv_s[...] = jnp.zeros_like(dv_s)

    def per_q(qb, _):
        q_start = (my_index ^ qb) * rows

        def doc_step(j, state):
            bound, first, lo = state
            bound = bound + lengths_ref[0, j]
            first = jnp.where(bound <= q_start, bound, first)
            t_pos = q_start + lax.broadcasted_iota(jnp.int32, (1, rows), 1)
            lo = jnp.where(bound <= t_pos, bound, lo)
            return bound, first, lo

        _, first, lo = lax.fori_loop(
            0, doc_count, doc_step, (jnp.int32(0), jnp.int32(0), jnp.zeros((1, rows), jnp.int32))
        )
        t_pos = q_start + lax.broadcasted_iota(jnp.int32, (1, rows), 1)
        m_s[...] = jnp.full_like(m_s, -jnp.inf)
        l_s[...] = jnp.zeros_like(l_s)
        w_s[...] = jnp.zeros_like(w_s)
        dqt_s[...] = jnp.zeros_like(dqt_s)

        def locate(j):
            kb = jnp.where(j < 2, j ^ qb, j)
            k_start = ((my_index ^ (kb & 1)) - (kb // 2) * 2) * rows
            live = (k_start >= 0) & (k_start <= q_start) & (k_start + rows > first)
            return kb, k_start, live

        def phase_a(j, _):
            kb, k_start, live = locate(j)

            @pl.when(live)
            def _():
                u_pos = k_start + lax.broadcasted_iota(jnp.int32, (rows, rows), 0)
                bias = jnp.where((u_pos >= lo) & (u_pos <= t_pos), 0.0, -jnp.inf)
                k = k_s[kb]
                v = v_s[kb]
                for h in range(GROUP):
                    s = nt(k, q_s[qb * GROUP + h]) * EXP2_SCALE + bias
                    dp = nt(v, g_s[qb * GROUP + h])
                    m_old = m_s[h]
                    m_new = jnp.maximum(m_old, jnp.max(s, axis=0, keepdims=True))
                    keep = jnp.exp2(m_old - m_new)
                    e = jnp.exp2(s - m_new)
                    l_s[h] = l_s[h] * keep + jnp.sum(e, axis=0, keepdims=True)
                    w_s[h] = w_s[h] * keep + jnp.sum(e * dp, axis=0, keepdims=True)
                    m_s[h] = m_new
                    mb_s[kb * GROUP + h] = m_new
                    e_s[kb * GROUP + h] = e
                    dp_s[kb * GROUP + h] = dp

            return 0

        lax.fori_loop(0, BLOCKS, phase_a, 0)

        def phase_b(j, _):
            kb, k_start, live = locate(j)

            @pl.when(live)
            def _():
                kt = kt_s[kb]
                dv = None
                dk = None
                for h in range(GROUP):
                    inverse = 1.0 / l_s[h]
                    grad_dot = w_s[h] * inverse
                    alpha = jnp.exp2(mb_s[kb * GROUP + h] - m_s[h]) * inverse
                    p = e_s[kb * GROUP + h] * alpha
                    ds = (p * (dp_s[kb * GROUP + h] - grad_dot)).astype(jnp.bfloat16)
                    dv_h = nn(p.astype(jnp.bfloat16), g_s[qb * GROUP + h])
                    dk_h = nn(ds, q_s[qb * GROUP + h])
                    dv = dv_h if dv is None else dv + dv_h
                    dk = dk_h if dk is None else dk + dk_h
                    dqt_s[h] += nn(kt, ds)
                dv_s[kb] += dv
                dk_s[kb] += dk

            return 0

        lax.fori_loop(0, BLOCKS, phase_b, 0)

        @pl.when(qb == 0)
        def _():
            for h in range(GROUP):
                own_dq[:, h * HD : (h + 1) * HD] = dqt_s[h].T.astype(own_dq.dtype)

        @pl.when(qb == 1)
        def _():
            for h in range(GROUP):
                sib_dq[:, h * HD : (h + 1) * HD] = dqt_s[h].T.astype(sib_dq.dtype)

        return 0

    lax.fori_loop(0, 2, per_q, 0)
    for d, out in enumerate((out0, out1, out2)):
        for p in range(2):
            out[0, p] = dk_s[2 * d + p].astype(out.dtype)
            out[1, p] = dv_s[2 * d + p].astype(out.dtype)


def grads_call(head, lengths, where, own_qg, sib_qg, kv0, kv1, kv2):
    rows = own_qg.shape[1]
    wide = GROUP * HD
    half = lambda part: pl.BlockSpec((None, rows, wide), lambda i, w: (part, 0, head))
    whole = pl.BlockSpec((2, 2, rows, HD), lambda i, w: (0, 0, 0, 0))
    dq_spec = pl.BlockSpec((rows, wide), lambda i, w: (0, 0))
    f32 = jnp.float32
    bf16 = jnp.bfloat16

    def kernel(where_ref, lengths_ref, *refs):
        grads_kernel(lengths_ref, where_ref, *refs)

    pair = 2 * GROUP
    tiles = BLOCKS * GROUP
    tile_work = 2 * rows * rows * HD
    return pl.pallas_call(
        kernel,
        grid_spec=pltpu.PrefetchScalarGridSpec(
            num_scalar_prefetch=1,
            grid=(1,),
            in_specs=[
                pl.BlockSpec(memory_space=pltpu.SMEM),
                half(0), half(0), half(1), half(1), whole, whole, whole,
            ],
            out_specs=[dq_spec, dq_spec, whole, whole, whole],
            scratch_shapes=[
                pltpu.VMEM((pair, rows, HD), bf16),
                pltpu.VMEM((pair, rows, HD), bf16),
                pltpu.VMEM((BLOCKS, rows, HD), bf16),
                pltpu.VMEM((BLOCKS, rows, HD), bf16),
                pltpu.VMEM((BLOCKS, HD, rows), bf16),
                pltpu.VMEM((tiles, rows, rows), f32),
                pltpu.VMEM((tiles, rows, rows), f32),
                pltpu.VMEM((tiles, 1, rows), f32),
                pltpu.VMEM((GROUP, 1, rows), f32),
                pltpu.VMEM((GROUP, 1, rows), f32),
                pltpu.VMEM((GROUP, 1, rows), f32),
                pltpu.VMEM((GROUP, HD, rows), f32),
                pltpu.VMEM((BLOCKS, rows, HD), f32),
                pltpu.VMEM((BLOCKS, rows, HD), f32),
            ],
        ),
        out_shape=[
            jax.ShapeDtypeStruct((rows, wide), bf16),
            jax.ShapeDtypeStruct((rows, wide), bf16),
            jax.ShapeDtypeStruct((2, 2, rows, HD), f32),
            jax.ShapeDtypeStruct((2, 2, rows, HD), bf16),
            jax.ShapeDtypeStruct((2, 2, rows, HD), bf16),
        ],
        compiler_params=pltpu.CompilerParams(vmem_limit_bytes=40 * 1024 * 1024),
        cost_estimate=pl.CostEstimate(
            flops=5 * 6 * GROUP * tile_work, transcendentals=6 * GROUP * rows * rows,
            bytes_accessed=6 * 1024 * 1024,
        ),
    )(where, lengths, own_qg, sib_qg, own_qg, sib_qg, kv0, kv1, kv2)


def body(query_rows, key_rows, value_rows, out_grad, lengths, loss_mask):
    rows = query_rows.shape[1]
    my_index = lax.axis_index("ctx")
    parity = my_index % 2
    shard_count = lax.axis_size("ctx")
    mask = loss_mask[0].astype(jnp.float32)
    count = everywhere_sum(jnp.broadcast_to(jnp.sum(mask), (8, 128)))[0, 0]
    loss_scale = lax.axis_size("dp") * rows * shard_count / count
    where = my_index.astype(jnp.int32).reshape(1)

    def halves(array):
        width = array.shape[-1] // 2
        mine = lax.dynamic_slice_in_dim(array, parity * width, width, array.ndim - 1)
        theirs = lax.dynamic_slice_in_dim(array, (1 - parity) * width, width, array.ndim - 1)
        return mine, theirs

    own_kv, give_kv = halves(jnp.stack([key_rows[0], value_rows[0]]))
    got_kv = swapped(give_kv, 1)
    local = [
        jnp.stack([own_kv[..., h * HD : (h + 1) * HD], got_kv[..., h * HD : (h + 1) * HD]], 1)
        for h in range(MINE)
    ]
    near = [shifted(kv, 2) for kv in local]
    far = [shifted(kv, 4) for kv in local]
    masked = out_grad[0] * mask[:, None].astype(jnp.bfloat16)
    own_qg, give_qg = halves(jnp.stack([query_rows[0], masked]))
    got_qg = swapped(give_qg, 1)

    own_dq = []
    sib_dq = []
    totals = []
    for h in range(MINE):
        dq_o, dq_s, d0, d1, d2 = grads_call(
            h, lengths, where, own_qg, got_qg, local[h], near[h], far[h]
        )
        own_dq.append(dq_o)
        sib_dq.append(dq_s)
        totals.append(
            d0 + shifted(d1, -2).astype(jnp.float32) + shifted(d2, -4).astype(jnp.float32)
        )
    own_dq = jnp.concatenate(own_dq, 1)
    got_dq = swapped(jnp.concatenate(sib_dq, 1), 1)
    total = jnp.concatenate(totals, -1)
    own_dkv = total[:, 0]
    got_dkv = swapped(total[:, 1].astype(jnp.bfloat16), 1).astype(jnp.float32)

    def joined(mine, theirs):
        mine = mine.astype(jnp.float32)
        theirs = theirs.astype(jnp.float32)
        return jnp.where(
            parity == 0,
            jnp.concatenate([mine, theirs], -1),
            jnp.concatenate([theirs, mine], -1),
        )

    score_scale = loss_scale * HD ** (-0.5)
    query_grad = (joined(own_dq, got_dq) * score_scale).astype(jnp.bfloat16)
    key_grad = (joined(own_dkv[0], got_dkv[0]) * score_scale).astype(jnp.bfloat16)
    value_grad = (joined(own_dkv[1], got_dkv[1]) * loss_scale).astype(jnp.bfloat16)
    return query_grad[None], key_grad[None], value_grad[None]


def solution(mesh):
    placed = (
        P("dp", "ctx", None),
        P("dp", "ctx", None),
        P("dp", "ctx", None),
        P("dp", "ctx", None),
        P("dp", None),
        P("dp", "ctx"),
    )
    return jax.shard_map(
        body,
        mesh=mesh,
        in_specs=placed,
        out_specs=(P("dp", "ctx", None), P("dp", "ctx", None), P("dp", "ctx", None)),
        check_vma=False,
    )
```

```python
import math

import jax
import jax.numpy as jnp
from jax import lax
from jax.experimental import pallas as pl
from jax.experimental.pallas import tpu as pltpu
from jax.sharding import PartitionSpec as P


HQ = 16
HK = 4
HD = 128
WIN = 4
GROUP = HQ // HK
MINE = HK // 2
BLOCKS = WIN + 2
EXP2_SCALE = HD ** (-0.5) * math.log2(math.e)


def shifted(value, by):
    count = lax.axis_size("ctx")
    pairs = [(i, i + by) for i in range(count) if 0 <= i + by < count]
    return lax.ppermute(value, "ctx", pairs)


def swapped(value, bit):
    count = lax.axis_size("ctx")
    return lax.ppermute(value, "ctx", [(i, i ^ bit) for i in range(count)])


def everywhere_sum(value):
    dp_count = lax.axis_size("dp")
    step = 1
    while step < dp_count:
        other = lax.ppermute(value, "dp", [(i, i ^ step) for i in range(dp_count)])
        value = value + other
        step *= 2
    step = 1
    while step < lax.axis_size("ctx"):
        other = swapped(value, step)
        value = value + other
        step *= 2
    return value


def nt(a, b):
    return lax.dot_general(a, b, (((1,), (1,)), ((), ())), preferred_element_type=jnp.float32)


def nn(a, b):
    return lax.dot_general(a, b, (((1,), (0,)), ((), ())), preferred_element_type=jnp.float32)


def mask_column(mask_ref):
    rows = mask_ref.shape[1]
    return jnp.broadcast_to(mask_ref[...].astype(jnp.float32), (HD, rows)).T


def in_vmem():
    return pl.BlockSpec(memory_space=pltpu.VMEM)


def simple_call(kernel, where, in_specs, out_shape, *args):
    if not isinstance(out_shape, (list, tuple)):
        out_shape = [out_shape]
    return pl.pallas_call(
        kernel,
        grid_spec=pltpu.PrefetchScalarGridSpec(
            num_scalar_prefetch=1,
            grid=(1,),
            in_specs=in_specs,
            out_specs=[in_vmem() for _ in out_shape],
        ),
        out_shape=out_shape,
        compiler_params=pltpu.CompilerParams(vmem_limit_bytes=8 * 1024 * 1024),
        cost_estimate=pl.CostEstimate(flops=0, transcendentals=0, bytes_accessed=1024 * 1024),
    )(where, *args)


def column_block(rows, width, pick):
    return pl.BlockSpec((None, rows, width), lambda i, w: (0, 0, pick(w[0])))


def give_kv_call(where, key_rows, value_rows):
    rows = key_rows.shape[1]
    width = MINE * HD

    def kernel(where_ref, k_ref, v_ref, out):
        for h in range(MINE):
            out[h, 0] = k_ref[:, h * HD : (h + 1) * HD]
            out[h, 1] = v_ref[:, h * HD : (h + 1) * HD]

    theirs = column_block(rows, width, lambda i: 1 - (i & 1))
    shape = jax.ShapeDtypeStruct((MINE, 2, rows, HD), jnp.bfloat16)
    return simple_call(kernel, where, [theirs, theirs], shape, key_rows, value_rows)[0]


def local_kv_call(where, key_rows, value_rows, got_kv):
    rows = key_rows.shape[1]
    width = MINE * HD

    def kernel(where_ref, k_ref, v_ref, got, *outs):
        for h, out in enumerate(outs):
            out[0, 0] = k_ref[:, h * HD : (h + 1) * HD]
            out[0, 1] = v_ref[:, h * HD : (h + 1) * HD]
            out[1] = got[h]

    own = column_block(rows, width, lambda i: i & 1)
    shape = [jax.ShapeDtypeStruct((2, 2, rows, HD), jnp.bfloat16) for _ in range(MINE)]
    return simple_call(kernel, where, [own, own, in_vmem()], shape, key_rows, value_rows, got_kv)


def give_qg_call(where, query_rows, out_grad, loss_mask, after):
    rows = query_rows.shape[1]
    width = MINE * GROUP * HD

    def kernel(where_ref, q_ref, g_ref, mask_ref, after_ref, out, token):
        keep_rows = mask_column(mask_ref)
        out[0] = q_ref[...]
        for h in range(MINE * GROUP):
            columns = slice(h * HD, (h + 1) * HD)
            out[1, :, columns] = (g_ref[:, columns].astype(jnp.float32) * keep_rows).astype(
                jnp.bfloat16
            )
        local = jnp.sum(mask_ref[...].astype(jnp.float32), axis=1, keepdims=True)
        token[...] = jnp.broadcast_to(local, token.shape)

    theirs = column_block(rows, width, lambda i: 1 - (i & 1))
    shape = [
        jax.ShapeDtypeStruct((2, rows, width), jnp.bfloat16),
        jax.ShapeDtypeStruct((8, HD), jnp.float32),
    ]
    return simple_call(
        kernel, where, [theirs, theirs, in_vmem(), pl.BlockSpec(memory_space=pl.ANY)], shape,
        query_rows, out_grad, loss_mask, after,
    )


def total_call(where, numerator, parts, count):
    rows = parts[0][0].shape[2]

    def kernel(where_ref, *refs):
        own, give = refs[-2:]
        scale = numerator / refs[-3][0:1, :]
        for h in range(MINE):
            d0, r1, r2 = refs[3 * h : 3 * h + 3]
            for kv, factor in enumerate((scale * HD ** (-0.5), scale)):
                for p, out in enumerate((own, give)):
                    out[h, kv] = (
                        (d0[p, kv] + r1[p, kv].astype(jnp.float32) + r2[p, kv].astype(jnp.float32))
                        * factor
                    ).astype(jnp.bfloat16)

    args = [a for part in parts for a in part] + [count]
    specs = [in_vmem() for _ in args]
    shape = [jax.ShapeDtypeStruct((MINE, 2, rows, HD), jnp.bfloat16)] * 2
    return simple_call(kernel, where, specs, shape, *args)


def finish_kv_call(where, own, got):
    rows = own.shape[2]
    width = MINE * HD

    def kernel(where_ref, own_ref, got_ref, *outs):
        parity = where_ref[0] & 1
        for kv, out in enumerate(outs):
            for h in range(MINE):
                mine = pl.multiple_of(parity * width + h * HD, HD)
                theirs = pl.multiple_of((1 - parity) * width + h * HD, HD)
                out[0, :, pl.ds(mine, HD)] = own_ref[h, kv]
                out[0, :, pl.ds(theirs, HD)] = got_ref[h, kv]

    shape = [jax.ShapeDtypeStruct((1, rows, 2 * width), jnp.bfloat16)] * 2
    return simple_call(kernel, where, [in_vmem()] * 2, shape, own, got)


def finish_q_call(where, numerator, own, got, count):
    rows = own[0].shape[0]
    wide = GROUP * HD
    width = MINE * wide

    def kernel(where_ref, *refs):
        own_refs = refs[:MINE]
        got_refs = refs[MINE : 2 * MINE]
        count_ref, out, token = refs[2 * MINE :]
        token[...] = count_ref[...]
        scale = numerator / count_ref[0:1, :] * HD ** (-0.5)
        parity = where_ref[0] & 1
        for base, parts in ((parity * width, own_refs), ((1 - parity) * width, got_refs)):
            for h, part in enumerate(parts):
                for j in range(GROUP):
                    at = pl.multiple_of(base + h * wide + j * HD, HD)
                    value = part[:, j * HD : (j + 1) * HD].astype(jnp.float32) * scale
                    out[0, :, pl.ds(at, HD)] = value.astype(out.dtype)

    shape = [
        jax.ShapeDtypeStruct((1, rows, 2 * width), jnp.bfloat16),
        jax.ShapeDtypeStruct(count.shape, count.dtype),
    ]
    args = list(own) + list(got) + [count]
    return simple_call(kernel, where, [in_vmem() for _ in args], shape, *args)


def grads_kernel(
    where_ref, lengths_ref, mask_ref, token_in, own_q, own_g, got_qg, kv0, kv1, kv2,
    own_dq, sib_dq, out0, out1, out2, token_out,
    q_s, g_s, k_s, v_s, kt_s, e_s, dp_s, mb_s, m_s, l_s, w_s, dqt_s, dk_s, dv_s,
):
    rows = own_q.shape[0]
    token_out[...] = token_in[...]
    keep_rows = mask_column(mask_ref)
    my_index = where_ref[0]
    doc_count = lengths_ref.shape[1]
    for h in range(GROUP):
        columns = slice(h * HD, (h + 1) * HD)
        q_s[h] = own_q[:, columns]
        q_s[GROUP + h] = got_qg[0, :, columns]
        g_s[h] = (own_g[:, columns].astype(jnp.float32) * keep_rows).astype(jnp.bfloat16)
        g_s[GROUP + h] = got_qg[1, :, columns]
    for d, kv in enumerate((kv0, kv1, kv2)):
        for p in range(2):
            k_s[2 * d + p] = kv[p, 0]
            v_s[2 * d + p] = kv[p, 1]
            kt_s[2 * d + p] = kv[p, 0].T
    dk_s[...] = jnp.zeros_like(dk_s)
    dv_s[...] = jnp.zeros_like(dv_s)

    def per_q(qb, _):
        q_start = (my_index ^ qb) * rows

        def doc_step(j, state):
            bound, first, lo = state
            bound = bound + lengths_ref[0, j]
            first = jnp.where(bound <= q_start, bound, first)
            t_pos = q_start + lax.broadcasted_iota(jnp.int32, (1, rows), 1)
            lo = jnp.where(bound <= t_pos, bound, lo)
            return bound, first, lo

        _, first, lo = lax.fori_loop(
            0, doc_count, doc_step, (jnp.int32(0), jnp.int32(0), jnp.zeros((1, rows), jnp.int32))
        )
        t_pos = q_start + lax.broadcasted_iota(jnp.int32, (1, rows), 1)
        m_s[...] = jnp.full_like(m_s, -jnp.inf)
        l_s[...] = jnp.zeros_like(l_s)
        w_s[...] = jnp.zeros_like(w_s)
        dqt_s[...] = jnp.zeros_like(dqt_s)

        def locate(j):
            kb = jnp.where(j < 2, j ^ qb, j)
            k_start = ((my_index ^ (kb & 1)) - (kb // 2) * 2) * rows
            live = (k_start >= 0) & (k_start <= q_start) & (k_start + rows > first)
            return kb, k_start, live

        def phase_a(j, _):
            kb, k_start, live = locate(j)

            @pl.when(live)
            def _():
                u_pos = k_start + lax.broadcasted_iota(jnp.int32, (rows, rows), 0)
                bias = jnp.where((u_pos >= lo) & (u_pos <= t_pos), 0.0, -jnp.inf)
                k = k_s[kb]
                v = v_s[kb]
                for h in range(GROUP):
                    s = nt(k, q_s[qb * GROUP + h]) * EXP2_SCALE + bias
                    dp = nt(v, g_s[qb * GROUP + h])
                    m_old = m_s[h]
                    m_new = jnp.maximum(m_old, jnp.max(s, axis=0, keepdims=True))
                    keep = jnp.exp2(m_old - m_new)
                    e = jnp.exp2(s - m_new)
                    l_s[h] = l_s[h] * keep + jnp.sum(e, axis=0, keepdims=True)
                    w_s[h] = w_s[h] * keep + jnp.sum(e * dp, axis=0, keepdims=True)
                    m_s[h] = m_new
                    mb_s[kb * GROUP + h] = m_new
                    e_s[kb * GROUP + h] = e
                    dp_s[kb * GROUP + h] = dp

            return 0

        lax.fori_loop(0, BLOCKS, phase_a, 0)

        def phase_b(j, _):
            kb, _, live = locate(j)

            @pl.when(live)
            def _():
                kt = kt_s[kb]
                dv = None
                dk = None
                for h in range(GROUP):
                    inverse = 1.0 / l_s[h]
                    grad_dot = w_s[h] * inverse
                    alpha = jnp.exp2(mb_s[kb * GROUP + h] - m_s[h]) * inverse
                    p = e_s[kb * GROUP + h] * alpha
                    ds = (p * (dp_s[kb * GROUP + h] - grad_dot)).astype(jnp.bfloat16)
                    dv_h = nn(p.astype(jnp.bfloat16), g_s[qb * GROUP + h])
                    dk_h = nn(ds, q_s[qb * GROUP + h])
                    dv = dv_h if dv is None else dv + dv_h
                    dk = dk_h if dk is None else dk + dk_h
                    dqt_s[h] += nn(kt, ds)
                dv_s[kb] += dv
                dk_s[kb] += dk

            return 0

        lax.fori_loop(0, BLOCKS, phase_b, 0)

        @pl.when(qb == 0)
        def _():
            for h in range(GROUP):
                own_dq[:, h * HD : (h + 1) * HD] = dqt_s[h].T.astype(own_dq.dtype)

        @pl.when(qb == 1)
        def _():
            for h in range(GROUP):
                sib_dq[:, h * HD : (h + 1) * HD] = dqt_s[h].T.astype(sib_dq.dtype)

        return 0

    lax.fori_loop(0, 2, per_q, 0)
    for d, out in enumerate((out0, out1, out2)):
        for p in range(2):
            out[p, 0] = dk_s[2 * d + p].astype(out.dtype)
            out[p, 1] = dv_s[2 * d + p].astype(out.dtype)


def grads_call(head, where, lengths, loss_mask, token, query_rows, out_grad, got_qg, kv0, kv1, kv2):
    rows = query_rows.shape[1]
    wide = GROUP * HD
    own = column_block(rows, wide, lambda i: (i & 1) * MINE + head)
    got = pl.BlockSpec((2, rows, wide), lambda i, w: (0, 0, head))
    f32 = jnp.float32
    bf16 = jnp.bfloat16
    pair = 2 * GROUP
    tiles = BLOCKS * GROUP
    tile_work = 2 * rows * rows * HD
    return pl.pallas_call(
        grads_kernel,
        grid_spec=pltpu.PrefetchScalarGridSpec(
            num_scalar_prefetch=1,
            grid=(1,),
            in_specs=[
                pl.BlockSpec(memory_space=pltpu.SMEM),
                in_vmem(), in_vmem(), own, own, got, in_vmem(), in_vmem(), in_vmem(),
            ],
            out_specs=[in_vmem() for _ in range(6)],
            scratch_shapes=[
                pltpu.VMEM((pair, rows, HD), bf16),
                pltpu.VMEM((pair, rows, HD), bf16),
                pltpu.VMEM((BLOCKS, rows, HD), bf16),
                pltpu.VMEM((BLOCKS, rows, HD), bf16),
                pltpu.VMEM((BLOCKS, HD, rows), bf16),
                pltpu.VMEM((tiles, rows, rows), f32),
                pltpu.VMEM((tiles, rows, rows), f32),
                pltpu.VMEM((tiles, 1, rows), f32),
                pltpu.VMEM((GROUP, 1, rows), f32),
                pltpu.VMEM((GROUP, 1, rows), f32),
                pltpu.VMEM((GROUP, 1, rows), f32),
                pltpu.VMEM((GROUP, HD, rows), f32),
                pltpu.VMEM((BLOCKS, rows, HD), f32),
                pltpu.VMEM((BLOCKS, rows, HD), f32),
            ],
        ),
        out_shape=[
            jax.ShapeDtypeStruct((rows, wide), bf16),
            jax.ShapeDtypeStruct((rows, wide), bf16),
            jax.ShapeDtypeStruct((2, 2, rows, HD), f32),
            jax.ShapeDtypeStruct((2, 2, rows, HD), bf16),
            jax.ShapeDtypeStruct((2, 2, rows, HD), bf16),
            jax.ShapeDtypeStruct((8, HD), f32),
        ],
        compiler_params=pltpu.CompilerParams(vmem_limit_bytes=26 * 1024 * 1024),
        name="grads",
        cost_estimate=pl.CostEstimate(
            flops=5 * 6 * GROUP * tile_work, transcendentals=6 * GROUP * rows * rows,
            bytes_accessed=6 * 1024 * 1024,
        ),
    )(where, lengths, loss_mask, token, query_rows, out_grad, got_qg, kv0, kv1, kv2)


def work(query_rows, key_rows, value_rows, out_grad, lengths, loss_mask):
    rows = query_rows.shape[1]
    numerator = float(lax.axis_size("dp") * rows * lax.axis_size("ctx"))
    where = lax.axis_index("ctx").astype(jnp.int32).reshape(1)

    give_kv = give_kv_call(where, key_rows, value_rows)
    got_kv = swapped(give_kv, 1)
    give_qg, token = give_qg_call(where, query_rows, out_grad, loss_mask, give_kv)
    got_qg = swapped(give_qg, 1)
    local = local_kv_call(where, key_rows, value_rows, got_kv)
    near = []
    far = []
    for kv in local:
        near.append(shifted(kv, 2))
        far.append(shifted(kv, 4))

    own_dq = []
    got_dq = []
    parts = []
    for h in range(MINE):
        dq_o, dq_s, d0, d1, d2, token = grads_call(
            h, where, lengths, loss_mask, token, query_rows, out_grad, got_qg,
            local[h], near[h], far[h],
        )
        own_dq.append(dq_o)
        r1 = shifted(d1, -2)
        r2 = shifted(d2, -4)
        parts.append((d0, r1, r2))
        got_dq.append(swapped(dq_s, 1))
    count = everywhere_sum(token)
    query_grad, count = finish_q_call(where, numerator, own_dq, got_dq, count)
    own_total, give_total = total_call(where, numerator, parts, count)
    key_grad, value_grad = finish_kv_call(where, own_total, swapped(give_total, 1))
    return query_grad, key_grad, value_grad


def solution(mesh):
    placed = (
        P("dp", "ctx", None),
        P("dp", "ctx", None),
        P("dp", "ctx", None),
        P("dp", "ctx", None),
        P("dp", None),
        P("dp", "ctx"),
    )
    return jax.shard_map(
        work,
        mesh=mesh,
        in_specs=placed,
        out_specs=(P("dp", "ctx", None), P("dp", "ctx", None), P("dp", "ctx", None)),
        check_vma=False,
    )
```

```python
import math

import jax
import jax.numpy as jnp
from jax import lax
from jax.experimental import pallas as pl
from jax.experimental.pallas import tpu as pltpu
from jax.sharding import PartitionSpec as P


HQ = 16
HK = 4
HD = 128
WIN = 4
GROUP = HQ // HK
MINE = HK // 2
BLOCKS = WIN + 2
EXP2_SCALE = HD ** (-0.5) * math.log2(math.e)


def shifted(value, by):
    count = lax.axis_size("ctx")
    pairs = [(i, i + by) for i in range(count) if 0 <= i + by < count]
    return lax.ppermute(value, "ctx", pairs)


def swapped(value, bit):
    count = lax.axis_size("ctx")
    return lax.ppermute(value, "ctx", [(i, i ^ bit) for i in range(count)])


def everywhere_sum(value):
    dp_count = lax.axis_size("dp")
    step = 1
    while step < dp_count:
        other = lax.ppermute(value, "dp", [(i, i ^ step) for i in range(dp_count)])
        value = value + other
        step *= 2
    step = 1
    while step < lax.axis_size("ctx"):
        other = swapped(value, step)
        value = value + other
        step *= 2
    return value


def nt(a, b):
    return lax.dot_general(a, b, (((1,), (1,)), ((), ())), preferred_element_type=jnp.float32)


def nn(a, b):
    return lax.dot_general(a, b, (((1,), (0,)), ((), ())), preferred_element_type=jnp.float32)


def mask_column(mask_ref):
    rows = mask_ref.shape[1]
    return jnp.broadcast_to(mask_ref[...].astype(jnp.float32), (HD, rows)).T


def in_vmem():
    return pl.BlockSpec(memory_space=pltpu.VMEM)


def simple_call(kernel, where, in_specs, out_shape, *args, scratch=(), vmem_mib=8):
    if not isinstance(out_shape, (list, tuple)):
        out_shape = [out_shape]
    return pl.pallas_call(
        kernel,
        grid_spec=pltpu.PrefetchScalarGridSpec(
            num_scalar_prefetch=1,
            grid=(1,),
            in_specs=in_specs,
            out_specs=[in_vmem() for _ in out_shape],
            scratch_shapes=scratch,
        ),
        out_shape=out_shape,
        compiler_params=pltpu.CompilerParams(vmem_limit_bytes=vmem_mib * 1024 * 1024),
        cost_estimate=pl.CostEstimate(flops=0, transcendentals=0, bytes_accessed=1024 * 1024),
    )(where, *args)


def in_hbm():
    return pl.BlockSpec(memory_space=pltpu.HBM)


def split_kv_call(where, key_rows, value_rows):
    rows = key_rows.shape[1]

    def kernel(where_ref, k_ref, v_ref, give, own, sems):
        parity = where_ref[0] & 1
        copies = []
        for base, out in ((1 - parity, give), (parity, own)):
            for h in range(MINE):
                columns = pl.ds(pl.multiple_of((base * MINE + h) * HD, HD), HD)
                for kv, source in enumerate((k_ref, v_ref)):
                    copies.append(
                        pltpu.make_async_copy(
                            source.at[0, :, columns], out.at[h, kv], sems.at[len(copies)]
                        )
                    )
        for copy in copies:
            copy.start()
        for copy in copies:
            copy.wait()

    shape = [jax.ShapeDtypeStruct((MINE, 2, rows, HD), jnp.bfloat16)] * 2
    return simple_call(
        kernel, where, [in_hbm(), in_hbm()], shape, key_rows, value_rows,
        scratch=[pltpu.SemaphoreType.DMA((4 * MINE,))],
    )


def local_kv_call(where, own_kv, got_kv):
    def kernel(where_ref, own, got, *outs):
        for h, out in enumerate(outs):
            out[0] = own[h]
            out[1] = got[h]

    shape = [jax.ShapeDtypeStruct((2,) + own_kv.shape[1:], jnp.bfloat16) for _ in range(MINE)]
    return simple_call(kernel, where, [in_vmem()] * 2, shape, own_kv, got_kv)


def split_qg_call(where, query_rows, out_grad, loss_mask, after):
    rows = query_rows.shape[1]
    width = MINE * GROUP * HD

    def kernel(where_ref, q_ref, g_ref, mask_ref, after_ref, give, own, token, g_s, sems):
        parity = where_ref[0] & 1
        pieces = []
        for i, (base, out) in enumerate(((1 - parity, give), (parity, own))):
            columns = pl.ds(pl.multiple_of(base * width, width), width)
            g_copy = pltpu.make_async_copy(g_ref.at[0, :, columns], g_s.at[i], sems.at[i, 0])
            q_copy = pltpu.make_async_copy(q_ref.at[0, :, columns], out.at[0], sems.at[i, 1])
            g_copy.start()
            q_copy.start()
            pieces.append((g_copy, q_copy, out))
        keep_rows = mask_column(mask_ref)
        local = jnp.sum(mask_ref[...].astype(jnp.float32), axis=1, keepdims=True)
        token[...] = jnp.broadcast_to(local, token.shape)
        for i, (g_copy, q_copy, out) in enumerate(pieces):
            g_copy.wait()
            for h in range(MINE * GROUP):
                columns = slice(h * HD, (h + 1) * HD)
                out[1, :, columns] = (g_s[i, :, columns].astype(jnp.float32) * keep_rows).astype(
                    jnp.bfloat16
                )
            q_copy.wait()

    shape = [
        jax.ShapeDtypeStruct((2, rows, width), jnp.bfloat16),
        jax.ShapeDtypeStruct((2, rows, width), jnp.bfloat16),
        jax.ShapeDtypeStruct((8, HD), jnp.float32),
    ]
    return simple_call(
        kernel, where, [in_hbm(), in_hbm(), in_vmem(), pl.BlockSpec(memory_space=pl.ANY)], shape,
        query_rows, out_grad, loss_mask, after,
        scratch=[pltpu.VMEM((2, rows, width), jnp.bfloat16), pltpu.SemaphoreType.DMA((2, 2))],
    )


def total_call(where, numerator, parts, count):
    rows = parts[0][0].shape[2]

    def kernel(where_ref, *refs):
        own, give = refs[-2:]
        scale = numerator / refs[-3][0:1, :]
        for h in range(MINE):
            d0, r1, r2 = refs[3 * h : 3 * h + 3]
            for kv, factor in enumerate((scale * HD ** (-0.5), scale)):
                for p, out in enumerate((own, give)):
                    out[h, kv] = (
                        (d0[p, kv] + r1[p, kv].astype(jnp.float32) + r2[p, kv].astype(jnp.float32))
                        * factor
                    ).astype(jnp.bfloat16)

    args = [a for part in parts for a in part] + [count]
    specs = [in_vmem() for _ in args]
    shape = [jax.ShapeDtypeStruct((MINE, 2, rows, HD), jnp.bfloat16)] * 2
    return simple_call(kernel, where, specs, shape, *args)


def finish_kv_call(where, own, got):
    rows = own.shape[2]
    width = MINE * HD

    def kernel(where_ref, own_ref, got_ref, *outs):
        parity = where_ref[0] & 1
        for kv, out in enumerate(outs):
            for h in range(MINE):
                mine = pl.multiple_of(parity * width + h * HD, HD)
                theirs = pl.multiple_of((1 - parity) * width + h * HD, HD)
                out[0, :, pl.ds(mine, HD)] = own_ref[h, kv]
                out[0, :, pl.ds(theirs, HD)] = got_ref[h, kv]

    shape = [jax.ShapeDtypeStruct((1, rows, 2 * width), jnp.bfloat16)] * 2
    return simple_call(kernel, where, [in_vmem()] * 2, shape, own, got)


def finish_q_call(where, numerator, own, got, count):
    rows = own[0].shape[0]
    wide = GROUP * HD
    width = MINE * wide

    def kernel(where_ref, *refs):
        own_refs = refs[:MINE]
        got_refs = refs[MINE : 2 * MINE]
        count_ref, out, token = refs[2 * MINE :]
        token[...] = count_ref[...]
        scale = numerator / count_ref[0:1, :] * HD ** (-0.5)
        parity = where_ref[0] & 1
        for base, parts in ((parity * width, own_refs), ((1 - parity) * width, got_refs)):
            for h, part in enumerate(parts):
                for j in range(GROUP):
                    at = pl.multiple_of(base + h * wide + j * HD, HD)
                    value = part[:, j * HD : (j + 1) * HD].astype(jnp.float32) * scale
                    out[0, :, pl.ds(at, HD)] = value.astype(out.dtype)

    shape = [
        jax.ShapeDtypeStruct((1, rows, 2 * width), jnp.bfloat16),
        jax.ShapeDtypeStruct(count.shape, count.dtype),
    ]
    args = list(own) + list(got) + [count]
    return simple_call(kernel, where, [in_vmem() for _ in args], shape, *args)


def grads_kernel(
    where_ref, lengths_ref, own_qg, got_qg, kv0, kv1, kv2,
    own_dq, sib_dq, out0, out1, out2,
    q_s, g_s, k_s, v_s, kt_s, e_s, dp_s, mb_s, m_s, l_s, w_s, dqt_s, dk_s, dv_s,
):
    rows = own_qg.shape[1]
    my_index = where_ref[0]
    doc_count = lengths_ref.shape[1]
    for h in range(GROUP):
        columns = slice(h * HD, (h + 1) * HD)
        at = slice(h * rows, (h + 1) * rows)
        q_s[0, at] = own_qg[0, :, columns]
        q_s[1, at] = got_qg[0, :, columns]
        g_s[0, at] = own_qg[1, :, columns]
        g_s[1, at] = got_qg[1, :, columns]
    for d, kv in enumerate((kv0, kv1, kv2)):
        for p in range(2):
            k_s[2 * d + p] = kv[p, 0]
            v_s[2 * d + p] = kv[p, 1]
            kt_s[2 * d + p] = kv[p, 0].T
    dk_s[...] = jnp.zeros_like(dk_s)
    dv_s[...] = jnp.zeros_like(dv_s)

    def per_q(qb, _):
        q_start = (my_index ^ qb) * rows

        def doc_step(j, state):
            bound, first, last, lo = state
            bound = bound + lengths_ref[0, j]
            first = jnp.where(bound <= q_start, bound, first)
            last = jnp.where(bound <= q_start + rows - 1, bound, last)
            t_pos = q_start + lax.broadcasted_iota(jnp.int32, (1, rows), 1)
            lo = jnp.where(bound <= t_pos, bound, lo)
            return bound, first, last, lo

        zero = jnp.int32(0)
        _, first, last, lo = lax.fori_loop(
            0, doc_count, doc_step, (zero, zero, zero, jnp.zeros((1, rows), jnp.int32))
        )
        t_pos = q_start + lax.broadcasted_iota(jnp.int32, (1, rows), 1)
        m_s[...] = jnp.full_like(m_s, -jnp.inf)
        l_s[...] = jnp.zeros_like(l_s)
        w_s[...] = jnp.zeros_like(w_s)
        dqt_s[...] = jnp.zeros_like(dqt_s)

        def locate(j):
            kb = jnp.where(j < 2, j ^ qb, j)
            k_start = ((my_index ^ (kb & 1)) - (kb // 2) * 2) * rows
            live = (k_start >= 0) & (k_start <= q_start) & (k_start + rows > first)
            return kb, k_start, live

        def phase_a(j, _):
            kb, k_start, live = locate(j)

            def scores(bias):
                k = k_s[kb]
                v = v_s[kb]
                for h in range(GROUP):
                    s = nt(k, q_s[qb, h * rows : (h + 1) * rows]) * EXP2_SCALE
                    if bias is not None:
                        s = s + bias
                    dp = nt(v, g_s[qb, h * rows : (h + 1) * rows])
                    m_old = m_s[h]
                    m_new = jnp.maximum(m_old, jnp.max(s, axis=0, keepdims=True))
                    keep = jnp.exp2(m_old - m_new)
                    e = jnp.exp2(s - m_new)
                    l_s[h] = l_s[h] * keep + jnp.sum(e, axis=0, keepdims=True)
                    w_s[h] = w_s[h] * keep + jnp.sum(e * dp, axis=0, keepdims=True)
                    m_s[h] = m_new
                    mb_s[kb * GROUP + h] = m_new
                    e_s[kb * GROUP + h] = e
                    dp_s[kb * GROUP + h] = dp

            full = (k_start < q_start) & (k_start >= last)

            @pl.when(live & full)
            def _():
                scores(None)

            @pl.when(live & jnp.logical_not(full))
            def _():
                u_pos = k_start + lax.broadcasted_iota(jnp.int32, (rows, rows), 0)
                scores(jnp.where((u_pos >= lo) & (u_pos <= t_pos), 0.0, -jnp.inf))

            return 0

        lax.fori_loop(0, BLOCKS, phase_a, 0)

        def phase_b(j, _):
            kb, _, live = locate(j)

            @pl.when(live)
            def _():
                p_all = []
                ds_all = []
                for h in range(GROUP):
                    inverse = 1.0 / l_s[h]
                    grad_dot = w_s[h] * inverse
                    alpha = jnp.exp2(mb_s[kb * GROUP + h] - m_s[h]) * inverse
                    p = e_s[kb * GROUP + h] * alpha
                    ds_all.append((p * (dp_s[kb * GROUP + h] - grad_dot)).astype(jnp.bfloat16))
                    p_all.append(p.astype(jnp.bfloat16))
                ds = jnp.concatenate(ds_all, 1)
                dv_s[kb] += nn(jnp.concatenate(p_all, 1), g_s[qb])
                dk_s[kb] += nn(ds, q_s[qb])
                dqt_s[...] += nn(kt_s[kb], ds)

            return 0

        lax.fori_loop(0, BLOCKS, phase_b, 0)

        @pl.when(qb == 0)
        def _():
            for h in range(GROUP):
                own_dq[:, h * HD : (h + 1) * HD] = dqt_s[:, h * rows : (h + 1) * rows].T.astype(own_dq.dtype)

        @pl.when(qb == 1)
        def _():
            for h in range(GROUP):
                sib_dq[:, h * HD : (h + 1) * HD] = dqt_s[:, h * rows : (h + 1) * rows].T.astype(sib_dq.dtype)

        return 0

    lax.fori_loop(0, 2, per_q, 0)
    for d, out in enumerate((out0, out1, out2)):
        for p in range(2):
            out[p, 0] = dk_s[2 * d + p].astype(out.dtype)
            out[p, 1] = dv_s[2 * d + p].astype(out.dtype)


def grads_call(head, where, lengths, own_qg, got_qg, kv0, kv1, kv2):
    rows = own_qg.shape[1]
    wide = GROUP * HD
    half = pl.BlockSpec((2, rows, wide), lambda i, w: (0, 0, head))
    f32 = jnp.float32
    bf16 = jnp.bfloat16
    tiles = BLOCKS * GROUP
    tile_work = 2 * rows * rows * HD
    return pl.pallas_call(
        grads_kernel,
        grid_spec=pltpu.PrefetchScalarGridSpec(
            num_scalar_prefetch=1,
            grid=(1,),
            in_specs=[
                pl.BlockSpec(memory_space=pltpu.SMEM),
                half, half, in_vmem(), in_vmem(), in_vmem(),
            ],
            out_specs=[in_vmem() for _ in range(5)],
            scratch_shapes=[
                pltpu.VMEM((2, GROUP * rows, HD), bf16),
                pltpu.VMEM((2, GROUP * rows, HD), bf16),
                pltpu.VMEM((BLOCKS, rows, HD), bf16),
                pltpu.VMEM((BLOCKS, rows, HD), bf16),
                pltpu.VMEM((BLOCKS, HD, rows), bf16),
                pltpu.VMEM((tiles, rows, rows), f32),
                pltpu.VMEM((tiles, rows, rows), f32),
                pltpu.VMEM((tiles, 1, rows), f32),
                pltpu.VMEM((GROUP, 1, rows), f32),
                pltpu.VMEM((GROUP, 1, rows), f32),
                pltpu.VMEM((GROUP, 1, rows), f32),
                pltpu.VMEM((HD, GROUP * rows), f32),
                pltpu.VMEM((BLOCKS, rows, HD), f32),
                pltpu.VMEM((BLOCKS, rows, HD), f32),
            ],
        ),
        out_shape=[
            jax.ShapeDtypeStruct((rows, wide), bf16),
            jax.ShapeDtypeStruct((rows, wide), bf16),
            jax.ShapeDtypeStruct((2, 2, rows, HD), f32),
            jax.ShapeDtypeStruct((2, 2, rows, HD), bf16),
            jax.ShapeDtypeStruct((2, 2, rows, HD), bf16),
        ],
        compiler_params=pltpu.CompilerParams(vmem_limit_bytes=26 * 1024 * 1024),
        name="grads",
        cost_estimate=pl.CostEstimate(
            flops=5 * 6 * GROUP * tile_work, transcendentals=6 * GROUP * rows * rows,
            bytes_accessed=6 * 1024 * 1024,
        ),
    )(where, lengths, own_qg, got_qg, kv0, kv1, kv2)


def work(query_rows, key_rows, value_rows, out_grad, lengths, loss_mask):
    rows = query_rows.shape[1]
    numerator = float(lax.axis_size("dp") * rows * lax.axis_size("ctx"))
    where = lax.axis_index("ctx").astype(jnp.int32).reshape(1)

    query_rows, key_rows, value_rows, out_grad = (
        pltpu.with_memory_space_constraint(x, pltpu.HBM)
        for x in (query_rows, key_rows, value_rows, out_grad)
    )
    give_kv, own_kv = split_kv_call(where, key_rows, value_rows)
    got_kv = swapped(give_kv, 1)
    give_qg, own_qg, token = split_qg_call(where, query_rows, out_grad, loss_mask, give_kv)
    got_qg = swapped(give_qg, 1)
    local = local_kv_call(where, own_kv, got_kv)
    near = []
    far = []
    for kv in local:
        near.append(shifted(kv, 2))
        far.append(shifted(kv, 4))

    own_dq = []
    got_dq = []
    parts = []
    for h in range(MINE):
        dq_o, dq_s, d0, d1, d2 = grads_call(
            h, where, lengths, own_qg, got_qg, local[h], near[h], far[h]
        )
        own_dq.append(dq_o)
        r1 = shifted(d1, -2)
        r2 = shifted(d2, -4)
        parts.append((d0, r1, r2))
        got_dq.append(swapped(dq_s, 1))
    count = everywhere_sum(token)
    query_grad, count = finish_q_call(where, numerator, own_dq, got_dq, count)
    own_total, give_total = total_call(where, numerator, parts, count)
    key_grad, value_grad = finish_kv_call(where, own_total, swapped(give_total, 1))
    return query_grad, key_grad, value_grad


def solution(mesh):
    placed = (
        P("dp", "ctx", None),
        P("dp", "ctx", None),
        P("dp", "ctx", None),
        P("dp", "ctx", None),
        P("dp", None),
        P("dp", "ctx"),
    )
    return jax.shard_map(
        work,
        mesh=mesh,
        in_specs=placed,
        out_specs=(P("dp", "ctx", None), P("dp", "ctx", None), P("dp", "ctx", None)),
        check_vma=False,
    )
```

```python
import math

import jax
import jax.numpy as jnp
from jax import lax
from jax.experimental import pallas as pl
from jax.experimental.pallas import tpu as pltpu
from jax.sharding import PartitionSpec as P


HQ = 16
HK = 4
HD = 128
WIN = 4
GROUP = HQ // HK
MINE = HK // 2
BLOCKS = WIN + 2
EXP2_SCALE = HD ** (-0.5) * math.log2(math.e)


def shifted(value, by):
    count = lax.axis_size("ctx")
    pairs = [(i, i + by) for i in range(count) if 0 <= i + by < count]
    return lax.ppermute(value, "ctx", pairs)


def swapped(value, bit):
    count = lax.axis_size("ctx")
    return lax.ppermute(value, "ctx", [(i, i ^ bit) for i in range(count)])


def everywhere_sum(value):
    count = lax.axis_size("ctx")
    steps = [2**k for k in range(1, count.bit_length() - 1)] + [1]
    for step in steps[:-1]:
        other = swapped(value, step)
        value = value + other
    dp_count = lax.axis_size("dp")
    for step in (2**k for k in range(dp_count.bit_length() - 1)):
        other = lax.ppermute(value, "dp", [(i, i ^ step) for i in range(dp_count)])
        value = value + other
    other = swapped(value, 1)
    return value + other


def nt(a, b):
    return lax.dot_general(a, b, (((1,), (1,)), ((), ())), preferred_element_type=jnp.float32)


def nn(a, b):
    return lax.dot_general(a, b, (((1,), (0,)), ((), ())), preferred_element_type=jnp.float32)


def mask_column(mask_ref):
    rows = mask_ref.shape[1]
    return jnp.broadcast_to(mask_ref[...].astype(jnp.float32), (HD, rows)).T


def in_vmem():
    return pl.BlockSpec(memory_space=pltpu.VMEM)


def simple_call(kernel, where, in_specs, out_shape, *args, scratch=(), vmem_mib=8):
    if not isinstance(out_shape, (list, tuple)):
        out_shape = [out_shape]
    return pl.pallas_call(
        kernel,
        grid_spec=pltpu.PrefetchScalarGridSpec(
            num_scalar_prefetch=1,
            grid=(1,),
            in_specs=in_specs,
            out_specs=[in_vmem() for _ in out_shape],
            scratch_shapes=scratch,
        ),
        out_shape=out_shape,
        compiler_params=pltpu.CompilerParams(vmem_limit_bytes=vmem_mib * 1024 * 1024),
        cost_estimate=pl.CostEstimate(flops=0, transcendentals=0, bytes_accessed=1024 * 1024),
    )(where, *args)


def in_hbm():
    return pl.BlockSpec(memory_space=pltpu.HBM)


def split_kv_call(where, key_rows, value_rows):
    rows = key_rows.shape[1]

    def kernel(where_ref, k_ref, v_ref, give, own, sems):
        parity = where_ref[0] & 1
        copies = []
        for base, out in ((1 - parity, give), (parity, own)):
            for h in range(MINE):
                columns = pl.ds(pl.multiple_of((base * MINE + h) * HD, HD), HD)
                for kv, source in enumerate((k_ref, v_ref)):
                    copies.append(
                        pltpu.make_async_copy(
                            source.at[0, :, columns], out.at[h, kv], sems.at[len(copies)]
                        )
                    )
        for copy in copies:
            copy.start()
        for copy in copies:
            copy.wait()

    shape = [jax.ShapeDtypeStruct((MINE, 2, rows, HD), jnp.bfloat16)] * 2
    return simple_call(
        kernel, where, [in_hbm(), in_hbm()], shape, key_rows, value_rows,
        scratch=[pltpu.SemaphoreType.DMA((4 * MINE,))],
    )


def local_kv_call(where, own_kv, got_kv):
    def kernel(where_ref, own, got, *outs):
        for h, out in enumerate(outs):
            out[0] = own[h]
            out[1] = got[h]

    shape = [jax.ShapeDtypeStruct((2,) + own_kv.shape[1:], jnp.bfloat16) for _ in range(MINE)]
    return simple_call(kernel, where, [in_vmem()] * 2, shape, own_kv, got_kv)


def split_qg_call(where, query_rows, out_grad, loss_mask, after):
    rows = query_rows.shape[1]
    width = MINE * GROUP * HD

    def kernel(where_ref, q_ref, g_ref, mask_ref, after_ref, give, own, token, g_s, sems):
        parity = where_ref[0] & 1
        pieces = []
        for i, (base, out) in enumerate(((1 - parity, give), (parity, own))):
            columns = pl.ds(pl.multiple_of(base * width, width), width)
            g_copy = pltpu.make_async_copy(g_ref.at[0, :, columns], g_s.at[i], sems.at[i, 0])
            q_copy = pltpu.make_async_copy(q_ref.at[0, :, columns], out.at[0], sems.at[i, 1])
            g_copy.start()
            q_copy.start()
            pieces.append((g_copy, q_copy, out))
        keep_rows = mask_column(mask_ref)
        local = jnp.sum(mask_ref[...].astype(jnp.float32), axis=1, keepdims=True)
        token[...] = jnp.broadcast_to(local, token.shape)
        for i, (g_copy, q_copy, out) in enumerate(pieces):
            g_copy.wait()
            for h in range(MINE * GROUP):
                columns = slice(h * HD, (h + 1) * HD)
                out[1, :, columns] = (g_s[i, :, columns].astype(jnp.float32) * keep_rows).astype(
                    jnp.bfloat16
                )
            q_copy.wait()

    shape = [
        jax.ShapeDtypeStruct((2, rows, width), jnp.bfloat16),
        jax.ShapeDtypeStruct((2, rows, width), jnp.bfloat16),
        jax.ShapeDtypeStruct((8, HD), jnp.float32),
    ]
    return simple_call(
        kernel, where, [in_hbm(), in_hbm(), in_vmem(), pl.BlockSpec(memory_space=pl.ANY)], shape,
        query_rows, out_grad, loss_mask, after,
        scratch=[pltpu.VMEM((2, rows, width), jnp.bfloat16), pltpu.SemaphoreType.DMA((2, 2))],
    )


def total_call(where, numerator, parts, count):
    rows = parts[0][0].shape[2]

    def kernel(where_ref, *refs):
        own, give = refs[-2:]
        scale = numerator / refs[-3][0:1, :]
        for h in range(MINE):
            d0, r1, r2 = refs[3 * h : 3 * h + 3]
            for kv, factor in enumerate((scale * HD ** (-0.5), scale)):
                for p, out in enumerate((own, give)):
                    out[h, kv] = (
                        (d0[p, kv] + r1[p, kv].astype(jnp.float32) + r2[p, kv].astype(jnp.float32))
                        * factor
                    ).astype(jnp.bfloat16)

    args = [a for part in parts for a in part] + [count]
    specs = [in_vmem() for _ in args]
    shape = [jax.ShapeDtypeStruct((MINE, 2, rows, HD), jnp.bfloat16)] * 2
    return simple_call(kernel, where, specs, shape, *args)


def finish_kv_call(where, own, got):
    rows = own.shape[2]
    width = MINE * HD

    def kernel(where_ref, own_ref, got_ref, *outs):
        parity = where_ref[0] & 1
        for kv, out in enumerate(outs):
            for h in range(MINE):
                mine = pl.multiple_of(parity * width + h * HD, HD)
                theirs = pl.multiple_of((1 - parity) * width + h * HD, HD)
                out[0, :, pl.ds(mine, HD)] = own_ref[h, kv]
                out[0, :, pl.ds(theirs, HD)] = got_ref[h, kv]

    shape = [jax.ShapeDtypeStruct((1, rows, 2 * width), jnp.bfloat16)] * 2
    return simple_call(kernel, where, [in_vmem()] * 2, shape, own, got)


def finish_q_call(where, numerator, own, got, count):
    rows = own[0].shape[0]
    wide = GROUP * HD
    width = MINE * wide

    def kernel(where_ref, *refs):
        own_refs = refs[:MINE]
        got_refs = refs[MINE : 2 * MINE]
        count_ref, out, token = refs[2 * MINE :]
        token[...] = count_ref[...]
        scale = numerator / count_ref[0:1, :] * HD ** (-0.5)
        parity = where_ref[0] & 1
        for base, parts in ((parity * width, own_refs), ((1 - parity) * width, got_refs)):
            for h, part in enumerate(parts):
                for j in range(GROUP):
                    at = pl.multiple_of(base + h * wide + j * HD, HD)
                    value = part[:, j * HD : (j + 1) * HD].astype(jnp.float32) * scale
                    out[0, :, pl.ds(at, HD)] = value.astype(out.dtype)

    shape = [
        jax.ShapeDtypeStruct((1, rows, 2 * width), jnp.bfloat16),
        jax.ShapeDtypeStruct(count.shape, count.dtype),
    ]
    args = list(own) + list(got) + [count]
    return simple_call(kernel, where, [in_vmem() for _ in args], shape, *args)


def grads_kernel(
    where_ref, lengths_ref, own_qg, got_qg, kv0, kv1, kv2,
    own_dq, sib_dq, out0, out1, out2,
    q_s, g_s, k_s, v_s, kt_s, e_s, dp_s, mb_s, m_s, l_s, w_s, dqt_s, dk_s, dv_s,
):
    rows = own_qg.shape[1]
    my_index = where_ref[0]
    doc_count = lengths_ref.shape[1]
    for h in range(GROUP):
        columns = slice(h * HD, (h + 1) * HD)
        at = slice(h * rows, (h + 1) * rows)
        q_s[0, at] = own_qg[0, :, columns]
        q_s[1, at] = got_qg[0, :, columns]
        g_s[0, at] = own_qg[1, :, columns]
        g_s[1, at] = got_qg[1, :, columns]
    for d, kv in enumerate((kv0, kv1, kv2)):
        for p in range(2):
            k_s[2 * d + p] = kv[p, 0]
            v_s[2 * d + p] = kv[p, 1]
            kt_s[2 * d + p] = kv[p, 0].T
    dk_s[...] = jnp.zeros_like(dk_s)
    dv_s[...] = jnp.zeros_like(dv_s)

    def per_q(qb, _):
        q_start = (my_index ^ qb) * rows

        def doc_step(j, state):
            bound, first, last, lo = state
            bound = bound + lengths_ref[0, j]
            first = jnp.where(bound <= q_start, bound, first)
            last = jnp.where(bound <= q_start + rows - 1, bound, last)
            t_pos = q_start + lax.broadcasted_iota(jnp.int32, (1, rows), 1)
            lo = jnp.where(bound <= t_pos, bound, lo)
            return bound, first, last, lo

        zero = jnp.int32(0)
        _, first, last, lo = lax.fori_loop(
            0, doc_count, doc_step, (zero, zero, zero, jnp.zeros((1, rows), jnp.int32))
        )
        t_pos = q_start + lax.broadcasted_iota(jnp.int32, (1, rows), 1)
        m_s[...] = jnp.full_like(m_s, -jnp.inf)
        l_s[...] = jnp.zeros_like(l_s)
        w_s[...] = jnp.zeros_like(w_s)
        dqt_s[...] = jnp.zeros_like(dqt_s)

        def locate(j):
            kb = jnp.where(j < 2, j ^ qb, j)
            k_start = ((my_index ^ (kb & 1)) - (kb // 2) * 2) * rows
            live = (k_start >= 0) & (k_start <= q_start) & (k_start + rows > first)
            return kb, k_start, live

        def phase_a(j, _):
            kb, k_start, live = locate(j)

            def scores(bias):
                k = k_s[kb]
                v = v_s[kb]
                for h in range(GROUP):
                    s = nt(k, q_s[qb, h * rows : (h + 1) * rows]) * EXP2_SCALE
                    if bias is not None:
                        s = s + bias
                    dp = nt(v, g_s[qb, h * rows : (h + 1) * rows])
                    m_old = m_s[h]
                    m_new = jnp.maximum(m_old, jnp.max(s, axis=0, keepdims=True))
                    keep = jnp.exp2(m_old - m_new)
                    e = jnp.exp2(s - m_new)
                    l_s[h] = l_s[h] * keep + jnp.sum(e, axis=0, keepdims=True)
                    w_s[h] = w_s[h] * keep + jnp.sum(e * dp, axis=0, keepdims=True)
                    m_s[h] = m_new
                    mb_s[kb * GROUP + h] = m_new
                    e_s[kb * GROUP + h] = e
                    dp_s[kb * GROUP + h] = dp

            full = (k_start < q_start) & (k_start >= last)

            @pl.when(live & full)
            def _():
                scores(None)

            @pl.when(live & jnp.logical_not(full))
            def _():
                u_pos = k_start + lax.broadcasted_iota(jnp.int32, (rows, rows), 0)
                scores(jnp.where((u_pos >= lo) & (u_pos <= t_pos), 0.0, -jnp.inf))

            return 0

        lax.fori_loop(0, BLOCKS, phase_a, 0)

        def phase_b(j, _):
            kb, _, live = locate(j)

            @pl.when(live)
            def _():
                p_all = []
                ds_all = []
                for h in range(GROUP):
                    inverse = 1.0 / l_s[h]
                    grad_dot = w_s[h] * inverse
                    alpha = jnp.exp2(mb_s[kb * GROUP + h] - m_s[h]) * inverse
                    p = e_s[kb * GROUP + h] * alpha
                    ds_all.append((p * (dp_s[kb * GROUP + h] - grad_dot)).astype(jnp.bfloat16))
                    p_all.append(p.astype(jnp.bfloat16))
                ds = jnp.concatenate(ds_all, 1)
                dv_s[kb] += nn(jnp.concatenate(p_all, 1), g_s[qb])
                dk_s[kb] += nn(ds, q_s[qb])
                dqt_s[...] += nn(kt_s[kb], ds)

            return 0

        lax.fori_loop(0, BLOCKS, phase_b, 0)

        @pl.when(qb == 0)
        def _():
            for h in range(GROUP):
                own_dq[:, h * HD : (h + 1) * HD] = dqt_s[:, h * rows : (h + 1) * rows].T.astype(own_dq.dtype)

        @pl.when(qb == 1)
        def _():
            for h in range(GROUP):
                sib_dq[:, h * HD : (h + 1) * HD] = dqt_s[:, h * rows : (h + 1) * rows].T.astype(sib_dq.dtype)

        return 0

    lax.fori_loop(0, 2, per_q, 0)
    for d, out in enumerate((out0, out1, out2)):
        for p in range(2):
            out[p, 0] = dk_s[2 * d + p].astype(out.dtype)
            out[p, 1] = dv_s[2 * d + p].astype(out.dtype)


def grads_call(head, where, lengths, own_qg, got_qg, kv0, kv1, kv2):
    rows = own_qg.shape[1]
    wide = GROUP * HD
    half = pl.BlockSpec((2, rows, wide), lambda i, w: (0, 0, head))
    f32 = jnp.float32
    bf16 = jnp.bfloat16
    tiles = BLOCKS * GROUP
    tile_work = 2 * rows * rows * HD
    return pl.pallas_call(
        grads_kernel,
        grid_spec=pltpu.PrefetchScalarGridSpec(
            num_scalar_prefetch=1,
            grid=(1,),
            in_specs=[
                pl.BlockSpec(memory_space=pltpu.SMEM),
                half, half, in_vmem(), in_vmem(), in_vmem(),
            ],
            out_specs=[in_vmem() for _ in range(5)],
            scratch_shapes=[
                pltpu.VMEM((2, GROUP * rows, HD), bf16),
                pltpu.VMEM((2, GROUP * rows, HD), bf16),
                pltpu.VMEM((BLOCKS, rows, HD), bf16),
                pltpu.VMEM((BLOCKS, rows, HD), bf16),
                pltpu.VMEM((BLOCKS, HD, rows), bf16),
                pltpu.VMEM((tiles, rows, rows), f32),
                pltpu.VMEM((tiles, rows, rows), f32),
                pltpu.VMEM((tiles, 1, rows), f32),
                pltpu.VMEM((GROUP, 1, rows), f32),
                pltpu.VMEM((GROUP, 1, rows), f32),
                pltpu.VMEM((GROUP, 1, rows), f32),
                pltpu.VMEM((HD, GROUP * rows), f32),
                pltpu.VMEM((BLOCKS, rows, HD), f32),
                pltpu.VMEM((BLOCKS, rows, HD), f32),
            ],
        ),
        out_shape=[
            jax.ShapeDtypeStruct((rows, wide), bf16),
            jax.ShapeDtypeStruct((rows, wide), bf16),
            jax.ShapeDtypeStruct((2, 2, rows, HD), f32),
            jax.ShapeDtypeStruct((2, 2, rows, HD), bf16),
            jax.ShapeDtypeStruct((2, 2, rows, HD), bf16),
        ],
        compiler_params=pltpu.CompilerParams(vmem_limit_bytes=26 * 1024 * 1024),
        name="grads",
        cost_estimate=pl.CostEstimate(
            flops=5 * 6 * GROUP * tile_work, transcendentals=6 * GROUP * rows * rows,
            bytes_accessed=6 * 1024 * 1024,
        ),
    )(where, lengths, own_qg, got_qg, kv0, kv1, kv2)


def work(query_rows, key_rows, value_rows, out_grad, lengths, loss_mask):
    rows = query_rows.shape[1]
    numerator = float(lax.axis_size("dp") * rows * lax.axis_size("ctx"))
    where = lax.axis_index("ctx").astype(jnp.int32).reshape(1)

    query_rows, key_rows, value_rows, out_grad = (
        pltpu.with_memory_space_constraint(x, pltpu.HBM)
        for x in (query_rows, key_rows, value_rows, out_grad)
    )
    give_kv, own_kv = split_kv_call(where, key_rows, value_rows)
    got_kv = swapped(give_kv, 1)
    give_qg, own_qg, token = split_qg_call(where, query_rows, out_grad, loss_mask, give_kv)
    got_qg = swapped(give_qg, 1)
    local = local_kv_call(where, own_kv, got_kv)
    near = []
    far = []
    for kv in local:
        near.append(shifted(kv, 2))
        far.append(shifted(kv, 4))

    own_dq = []
    got_dq = []
    parts = []
    for h in range(MINE):
        dq_o, dq_s, d0, d1, d2 = grads_call(
            h, where, lengths, own_qg, got_qg, local[h], near[h], far[h]
        )
        own_dq.append(dq_o)
        r1 = shifted(d1, -2)
        r2 = shifted(d2, -4)
        parts.append((d0, r1, r2))
        got_dq.append(swapped(dq_s, 1))
    count = everywhere_sum(token)
    query_grad, count = finish_q_call(where, numerator, own_dq, got_dq, count)
    own_total, give_total = total_call(where, numerator, parts, count)
    key_grad, value_grad = finish_kv_call(where, own_total, swapped(give_total, 1))
    return query_grad, key_grad, value_grad


def solution(mesh):
    placed = (
        P("dp", "ctx", None),
        P("dp", "ctx", None),
        P("dp", "ctx", None),
        P("dp", "ctx", None),
        P("dp", None),
        P("dp", "ctx"),
    )
    return jax.shard_map(
        work,
        mesh=mesh,
        in_specs=placed,
        out_specs=(P("dp", "ctx", None), P("dp", "ctx", None), P("dp", "ctx", None)),
        check_vma=False,
    )
```

```python
import math

import jax
import jax.numpy as jnp
from jax import lax
from jax.experimental import pallas as pl
from jax.experimental.pallas import tpu as pltpu
from jax.sharding import PartitionSpec as P


HQ = 16
HK = 4
HD = 128
WIN = 4
GROUP = HQ // HK
MINE = HK // 2
BLOCKS = WIN + 2
EXP2_SCALE = HD ** (-0.5) * math.log2(math.e)


def shifted(value, by):
    count = lax.axis_size("ctx")
    pairs = [(i, i + by) for i in range(count) if 0 <= i + by < count]
    return lax.ppermute(value, "ctx", pairs)


def swapped(value, bit):
    count = lax.axis_size("ctx")
    return lax.ppermute(value, "ctx", [(i, i ^ bit) for i in range(count)])


def everywhere_sum(value):
    count = lax.axis_size("ctx")
    steps = [2**k for k in range(1, count.bit_length() - 1)] + [1]
    for step in steps[:-1]:
        other = swapped(value, step)
        value = value + other
    dp_count = lax.axis_size("dp")
    for step in (2**k for k in range(dp_count.bit_length() - 1)):
        other = lax.ppermute(value, "dp", [(i, i ^ step) for i in range(dp_count)])
        value = value + other
    other = swapped(value, 1)
    return value + other


def nt(a, b):
    return lax.dot_general(a, b, (((1,), (1,)), ((), ())), preferred_element_type=jnp.float32)


def nn(a, b):
    return lax.dot_general(a, b, (((1,), (0,)), ((), ())), preferred_element_type=jnp.float32)


def mask_column(mask_ref):
    rows = mask_ref.shape[1]
    return jnp.broadcast_to(mask_ref[...].astype(jnp.float32), (HD, rows)).T


def in_vmem():
    return pl.BlockSpec(memory_space=pltpu.VMEM)


def simple_call(kernel, where, in_specs, out_shape, *args, scratch=(), vmem_mib=8):
    if not isinstance(out_shape, (list, tuple)):
        out_shape = [out_shape]
    return pl.pallas_call(
        kernel,
        grid_spec=pltpu.PrefetchScalarGridSpec(
            num_scalar_prefetch=1,
            grid=(1,),
            in_specs=in_specs,
            out_specs=[in_vmem() for _ in out_shape],
            scratch_shapes=scratch,
        ),
        out_shape=out_shape,
        compiler_params=pltpu.CompilerParams(vmem_limit_bytes=vmem_mib * 1024 * 1024),
        cost_estimate=pl.CostEstimate(flops=0, transcendentals=0, bytes_accessed=1024 * 1024),
    )(where, *args)


def in_hbm():
    return pl.BlockSpec(memory_space=pltpu.HBM)


def split_kv_call(where, key_rows, value_rows):
    rows = key_rows.shape[1]

    def kernel(where_ref, k_ref, v_ref, give, own, sems):
        parity = where_ref[0] & 1
        copies = []
        for base, out in ((1 - parity, give), (parity, own)):
            for h in range(MINE):
                columns = pl.ds(pl.multiple_of((base * MINE + h) * HD, HD), HD)
                for kv, source in enumerate((k_ref, v_ref)):
                    copies.append(
                        pltpu.make_async_copy(
                            source.at[0, :, columns], out.at[h, kv], sems.at[len(copies)]
                        )
                    )
        for copy in copies:
            copy.start()
        for copy in copies:
            copy.wait()

    shape = [jax.ShapeDtypeStruct((MINE, 2, rows, HD), jnp.bfloat16)] * 2
    return simple_call(
        kernel, where, [in_hbm(), in_hbm()], shape, key_rows, value_rows,
        scratch=[pltpu.SemaphoreType.DMA((4 * MINE,))],
    )


def local_kv_call(where, own_kv, got_kv):
    def kernel(where_ref, own, got, *outs):
        for h, out in enumerate(outs):
            out[0] = own[h]
            out[1] = got[h]

    shape = [jax.ShapeDtypeStruct((2,) + own_kv.shape[1:], jnp.bfloat16) for _ in range(MINE)]
    return simple_call(kernel, where, [in_vmem()] * 2, shape, own_kv, got_kv)


def split_qg_call(where, query_rows, out_grad, loss_mask, after):
    rows = query_rows.shape[1]
    heads = MINE * GROUP
    width = heads * HD

    def kernel(where_ref, q_ref, g_ref, mask_ref, after_ref, give, own, token, g_s, sems):
        parity = where_ref[0] & 1
        pieces = []
        for i, (base, out) in enumerate(((1 - parity, give), (parity, own))):
            columns = pl.ds(pl.multiple_of(base * width, width), width)
            g_copy = pltpu.make_async_copy(g_ref.at[0, :, columns], g_s.at[i], sems.at[i, 0])
            g_copy.start()
            q_copies = []
            for h in range(heads):
                one = pl.ds(pl.multiple_of(base * width + h * HD, HD), HD)
                q_copies.append(
                    pltpu.make_async_copy(q_ref.at[0, :, one], out.at[0, h], sems.at[i, 1 + h])
                )
                q_copies[-1].start()
            pieces.append((g_copy, q_copies, out))
        keep_rows = mask_column(mask_ref)
        local = jnp.sum(mask_ref[...].astype(jnp.float32), axis=1, keepdims=True)
        token[...] = jnp.broadcast_to(local, token.shape)
        for i, (g_copy, q_copies, out) in enumerate(pieces):
            g_copy.wait()
            for h in range(heads):
                columns = slice(h * HD, (h + 1) * HD)
                out[1, h] = (g_s[i, :, columns].astype(jnp.float32) * keep_rows).astype(
                    jnp.bfloat16
                )
            for copy in q_copies:
                copy.wait()

    shape = [
        jax.ShapeDtypeStruct((2, heads, rows, HD), jnp.bfloat16),
        jax.ShapeDtypeStruct((2, heads, rows, HD), jnp.bfloat16),
        jax.ShapeDtypeStruct((8, HD), jnp.float32),
    ]
    return simple_call(
        kernel, where, [in_hbm(), in_hbm(), in_vmem(), pl.BlockSpec(memory_space=pl.ANY)], shape,
        query_rows, out_grad, loss_mask, after,
        scratch=[pltpu.VMEM((2, rows, width), jnp.bfloat16), pltpu.SemaphoreType.DMA((2, 1 + heads))],
    )


def total_call(where, numerator, parts, count):
    rows = parts[0][0].shape[2]

    def kernel(where_ref, *refs):
        own, give = refs[-2:]
        scale = numerator / refs[-3][0:1, :]
        for h in range(MINE):
            d0, r1, r2 = refs[3 * h : 3 * h + 3]
            for kv, factor in enumerate((scale * HD ** (-0.5), scale)):
                for p, out in enumerate((own, give)):
                    out[h, kv] = (
                        (d0[p, kv] + r1[p, kv].astype(jnp.float32) + r2[p, kv].astype(jnp.float32))
                        * factor
                    ).astype(jnp.bfloat16)

    args = [a for part in parts for a in part] + [count]
    specs = [in_vmem() for _ in args]
    shape = [jax.ShapeDtypeStruct((MINE, 2, rows, HD), jnp.bfloat16)] * 2
    return simple_call(kernel, where, specs, shape, *args)


def finish_kv_call(where, own, got):
    rows = own.shape[2]
    width = MINE * HD

    def kernel(where_ref, own_ref, got_ref, *outs):
        parity = where_ref[0] & 1
        for kv, out in enumerate(outs):
            for h in range(MINE):
                mine = pl.multiple_of(parity * width + h * HD, HD)
                theirs = pl.multiple_of((1 - parity) * width + h * HD, HD)
                out[0, :, pl.ds(mine, HD)] = own_ref[h, kv]
                out[0, :, pl.ds(theirs, HD)] = got_ref[h, kv]

    shape = [jax.ShapeDtypeStruct((1, rows, 2 * width), jnp.bfloat16)] * 2
    return simple_call(kernel, where, [in_vmem()] * 2, shape, own, got)


def finish_q_call(where, numerator, own, got, count):
    rows = own[0].shape[0]
    wide = GROUP * HD
    width = MINE * wide

    def kernel(where_ref, *refs):
        own_refs = refs[:MINE]
        got_refs = refs[MINE : 2 * MINE]
        count_ref, out, token = refs[2 * MINE :]
        token[...] = count_ref[...]
        scale = numerator / count_ref[0:1, :] * HD ** (-0.5)
        parity = where_ref[0] & 1
        for base, parts in ((parity * width, own_refs), ((1 - parity) * width, got_refs)):
            for h, part in enumerate(parts):
                for j in range(GROUP):
                    at = pl.multiple_of(base + h * wide + j * HD, HD)
                    value = part[:, j * HD : (j + 1) * HD].astype(jnp.float32) * scale
                    out[0, :, pl.ds(at, HD)] = value.astype(out.dtype)

    shape = [
        jax.ShapeDtypeStruct((1, rows, 2 * width), jnp.bfloat16),
        jax.ShapeDtypeStruct(count.shape, count.dtype),
    ]
    args = list(own) + list(got) + [count]
    return simple_call(kernel, where, [in_vmem() for _ in args], shape, *args)


def grads_kernel(
    where_ref, lengths_ref, own_qg, got_qg, kv0, kv1, kv2,
    own_dq, sib_dq, out0, out1, out2,
    k_s, v_s, kt_s, e_s, dp_s, mb_s, m_s, l_s, w_s, dqt_s, dk_s, dv_s,
):
    rows = own_qg.shape[2]
    my_index = where_ref[0]
    doc_count = lengths_ref.shape[1]
    for d, kv in enumerate((kv0, kv1, kv2)):
        for p in range(2):
            k_s[2 * d + p] = kv[p, 0]
            v_s[2 * d + p] = kv[p, 1]
            kt_s[2 * d + p] = kv[p, 0].T
    dk_s[...] = jnp.zeros_like(dk_s)
    dv_s[...] = jnp.zeros_like(dv_s)

    def per_q(qb, qg, dq):
        q_s, g_s = qg.at[0], qg.at[1]
        q_start = (my_index ^ qb) * rows

        def doc_step(j, state):
            bound, first, last, lo = state
            bound = bound + lengths_ref[0, j]
            first = jnp.where(bound <= q_start, bound, first)
            last = jnp.where(bound <= q_start + rows - 1, bound, last)
            t_pos = q_start + lax.broadcasted_iota(jnp.int32, (1, rows), 1)
            lo = jnp.where(bound <= t_pos, bound, lo)
            return bound, first, last, lo

        zero = jnp.int32(0)
        _, first, last, lo = lax.fori_loop(
            0, doc_count, doc_step, (zero, zero, zero, jnp.zeros((1, rows), jnp.int32))
        )
        t_pos = q_start + lax.broadcasted_iota(jnp.int32, (1, rows), 1)
        m_s[...] = jnp.full_like(m_s, -jnp.inf)
        l_s[...] = jnp.zeros_like(l_s)
        w_s[...] = jnp.zeros_like(w_s)
        dqt_s[...] = jnp.zeros_like(dqt_s)

        def locate(j):
            kb = jnp.where(j < 2, j ^ qb, j)
            k_start = ((my_index ^ (kb & 1)) - (kb // 2) * 2) * rows
            live = (k_start >= 0) & (k_start <= q_start) & (k_start + rows > first)
            return kb, k_start, live

        def phase_a(j, _):
            kb, k_start, live = locate(j)

            def scores(bias):
                k = k_s[kb]
                v = v_s[kb]
                for h in range(GROUP):
                    s = nt(k, q_s[h])
                    if bias is not None:
                        s = s + bias
                    dp = nt(v, g_s[h])
                    m_old = m_s[h]
                    m_new = jnp.maximum(m_old, jnp.max(s, axis=0, keepdims=True))
                    keep = jnp.exp2((m_old - m_new) * EXP2_SCALE)
                    e = jnp.exp2((s - m_new) * EXP2_SCALE)
                    l_s[h] = l_s[h] * keep + jnp.sum(e, axis=0, keepdims=True)
                    w_s[h] = w_s[h] * keep + jnp.sum(e * dp, axis=0, keepdims=True)
                    m_s[h] = m_new
                    mb_s[kb * GROUP + h] = m_new
                    e_s[kb * GROUP + h] = e
                    dp_s[kb * GROUP + h] = dp

            full = (k_start < q_start) & (k_start >= last)

            @pl.when(live & full)
            def _():
                scores(None)

            @pl.when(live & jnp.logical_not(full))
            def _():
                u_pos = k_start + lax.broadcasted_iota(jnp.int32, (rows, rows), 0)
                scores(jnp.where((u_pos >= lo) & (u_pos <= t_pos), 0.0, -jnp.inf))

            return 0

        lax.fori_loop(0, BLOCKS, phase_a, 0)

        def phase_b(j, _):
            kb, _, live = locate(j)

            @pl.when(live)
            def _():
                p_all = []
                ds_all = []
                for h in range(GROUP):
                    inverse = 1.0 / l_s[h]
                    grad_dot = w_s[h] * inverse
                    alpha = jnp.exp2((mb_s[kb * GROUP + h] - m_s[h]) * EXP2_SCALE) * inverse
                    p = e_s[kb * GROUP + h] * alpha
                    ds_all.append((p * (dp_s[kb * GROUP + h] - grad_dot)).astype(jnp.bfloat16))
                    p_all.append(p.astype(jnp.bfloat16))
                ds = jnp.concatenate(ds_all, 1)
                dv_s[kb] += nn(jnp.concatenate(p_all, 1), g_s[...].reshape(GROUP * rows, HD))
                dk_s[kb] += nn(ds, q_s[...].reshape(GROUP * rows, HD))
                dqt_s[...] += nn(kt_s[kb], ds)

            return 0

        lax.fori_loop(0, BLOCKS, phase_b, 0)

        for h in range(GROUP):
            dq[:, h * HD : (h + 1) * HD] = dqt_s[:, h * rows : (h + 1) * rows].T.astype(dq.dtype)

    per_q(0, own_qg, own_dq)
    per_q(1, got_qg, sib_dq)
    for d, out in enumerate((out0, out1, out2)):
        for p in range(2):
            out[p, 0] = dk_s[2 * d + p].astype(out.dtype)
            out[p, 1] = dv_s[2 * d + p].astype(out.dtype)


def grads_call(head, where, lengths, own_qg, got_qg, kv0, kv1, kv2):
    rows = own_qg.shape[2]
    wide = GROUP * HD
    half = pl.BlockSpec((2, GROUP, rows, HD), lambda i, w: (0, head, 0, 0))
    f32 = jnp.float32
    bf16 = jnp.bfloat16
    tiles = BLOCKS * GROUP
    tile_work = 2 * rows * rows * HD
    return pl.pallas_call(
        grads_kernel,
        grid_spec=pltpu.PrefetchScalarGridSpec(
            num_scalar_prefetch=1,
            grid=(1,),
            in_specs=[
                pl.BlockSpec(memory_space=pltpu.SMEM),
                half, half, in_vmem(), in_vmem(), in_vmem(),
            ],
            out_specs=[in_vmem() for _ in range(5)],
            scratch_shapes=[
                pltpu.VMEM((BLOCKS, rows, HD), bf16),
                pltpu.VMEM((BLOCKS, rows, HD), bf16),
                pltpu.VMEM((BLOCKS, HD, rows), bf16),
                pltpu.VMEM((tiles, rows, rows), f32),
                pltpu.VMEM((tiles, rows, rows), f32),
                pltpu.VMEM((tiles, 1, rows), f32),
                pltpu.VMEM((GROUP, 1, rows), f32),
                pltpu.VMEM((GROUP, 1, rows), f32),
                pltpu.VMEM((GROUP, 1, rows), f32),
                pltpu.VMEM((HD, GROUP * rows), f32),
                pltpu.VMEM((BLOCKS, rows, HD), f32),
                pltpu.VMEM((BLOCKS, rows, HD), f32),
            ],
        ),
        out_shape=[
            jax.ShapeDtypeStruct((rows, wide), bf16),
            jax.ShapeDtypeStruct((rows, wide), bf16),
            jax.ShapeDtypeStruct((2, 2, rows, HD), f32),
            jax.ShapeDtypeStruct((2, 2, rows, HD), bf16),
            jax.ShapeDtypeStruct((2, 2, rows, HD), bf16),
        ],
        compiler_params=pltpu.CompilerParams(vmem_limit_bytes=26 * 1024 * 1024),
        name="grads",
        cost_estimate=pl.CostEstimate(
            flops=5 * 6 * GROUP * tile_work, transcendentals=6 * GROUP * rows * rows,
            bytes_accessed=6 * 1024 * 1024,
        ),
    )(where, lengths, own_qg, got_qg, kv0, kv1, kv2)


def work(query_rows, key_rows, value_rows, out_grad, lengths, loss_mask):
    rows = query_rows.shape[1]
    numerator = float(lax.axis_size("dp") * rows * lax.axis_size("ctx"))
    where = lax.axis_index("ctx").astype(jnp.int32).reshape(1)

    query_rows, key_rows, value_rows, out_grad = (
        pltpu.with_memory_space_constraint(x, pltpu.HBM)
        for x in (query_rows, key_rows, value_rows, out_grad)
    )
    give_kv, own_kv = split_kv_call(where, key_rows, value_rows)
    got_kv = swapped(give_kv, 1)
    give_qg, own_qg, token = split_qg_call(where, query_rows, out_grad, loss_mask, give_kv)
    got_qg = swapped(give_qg, 1)
    local = local_kv_call(where, own_kv, got_kv)
    near = []
    far = []
    for kv in local:
        near.append(shifted(kv, 2))
        far.append(shifted(kv, 4))

    own_dq = []
    got_dq = []
    parts = []
    for h in range(MINE):
        dq_o, dq_s, d0, d1, d2 = grads_call(
            h, where, lengths, own_qg, got_qg, local[h], near[h], far[h]
        )
        own_dq.append(dq_o)
        r1 = shifted(d1, -2)
        r2 = shifted(d2, -4)
        parts.append((d0, r1, r2))
        got_dq.append(swapped(dq_s, 1))
    count = everywhere_sum(token)
    query_grad, count = finish_q_call(where, numerator, own_dq, got_dq, count)
    own_total, give_total = total_call(where, numerator, parts, count)
    key_grad, value_grad = finish_kv_call(where, own_total, swapped(give_total, 1))
    return query_grad, key_grad, value_grad


def solution(mesh):
    placed = (
        P("dp", "ctx", None),
        P("dp", "ctx", None),
        P("dp", "ctx", None),
        P("dp", "ctx", None),
        P("dp", None),
        P("dp", "ctx"),
    )
    return jax.shard_map(
        work,
        mesh=mesh,
        in_specs=placed,
        out_specs=(P("dp", "ctx", None), P("dp", "ctx", None), P("dp", "ctx", None)),
        check_vma=False,
    )
```

```python
import math

import jax
import jax.numpy as jnp
from jax import lax
from jax.experimental import pallas as pl
from jax.experimental.pallas import tpu as pltpu
from jax.sharding import PartitionSpec as P


HQ = 16
HK = 4
HD = 128
WIN = 4
GROUP = HQ // HK
MINE = HK // 2
BLOCKS = WIN + 2
EXP2_SCALE = HD ** (-0.5) * math.log2(math.e)
MOST_EXCESS = 60.0


def shifted(value, by):
    count = lax.axis_size("ctx")
    pairs = [(i, i + by) for i in range(count) if 0 <= i + by < count]
    return lax.ppermute(value, "ctx", pairs)


def swapped(value, bit):
    count = lax.axis_size("ctx")
    return lax.ppermute(value, "ctx", [(i, i ^ bit) for i in range(count)])


def everywhere_sum(value):
    count = lax.axis_size("ctx")
    steps = [2**k for k in range(1, count.bit_length() - 1)] + [1]
    for step in steps[:-1]:
        other = swapped(value, step)
        value = value + other
    dp_count = lax.axis_size("dp")
    for step in (2**k for k in range(dp_count.bit_length() - 1)):
        other = lax.ppermute(value, "dp", [(i, i ^ step) for i in range(dp_count)])
        value = value + other
    other = swapped(value, 1)
    return value + other


def nt(a, b):
    return lax.dot_general(a, b, (((1,), (1,)), ((), ())), preferred_element_type=jnp.float32)


def nn(a, b):
    return lax.dot_general(a, b, (((1,), (0,)), ((), ())), preferred_element_type=jnp.float32)


def mask_column(mask_ref):
    rows = mask_ref.shape[1]
    return jnp.broadcast_to(mask_ref[...].astype(jnp.float32), (HD, rows)).T


def in_vmem():
    return pl.BlockSpec(memory_space=pltpu.VMEM)


def simple_call(kernel, where, in_specs, out_shape, *args, scratch=(), vmem_mib=8):
    if not isinstance(out_shape, (list, tuple)):
        out_shape = [out_shape]
    return pl.pallas_call(
        kernel,
        grid_spec=pltpu.PrefetchScalarGridSpec(
            num_scalar_prefetch=1,
            grid=(1,),
            in_specs=in_specs,
            out_specs=[in_vmem() for _ in out_shape],
            scratch_shapes=scratch,
        ),
        out_shape=out_shape,
        compiler_params=pltpu.CompilerParams(vmem_limit_bytes=vmem_mib * 1024 * 1024),
        cost_estimate=pl.CostEstimate(flops=0, transcendentals=0, bytes_accessed=1024 * 1024),
    )(where, *args)


def in_hbm():
    return pl.BlockSpec(memory_space=pltpu.HBM)


def split_kv_call(where, key_rows, value_rows):
    rows = key_rows.shape[1]

    def kernel(where_ref, k_ref, v_ref, give, own, sems):
        parity = where_ref[0] & 1
        copies = []
        for base, out in ((1 - parity, give), (parity, own)):
            for h in range(MINE):
                columns = pl.ds(pl.multiple_of((base * MINE + h) * HD, HD), HD)
                for kv, source in enumerate((k_ref, v_ref)):
                    copies.append(
                        pltpu.make_async_copy(
                            source.at[0, :, columns], out.at[h, kv], sems.at[len(copies)]
                        )
                    )
        for copy in copies:
            copy.start()
        for copy in copies:
            copy.wait()

    shape = [jax.ShapeDtypeStruct((MINE, 2, rows, HD), jnp.bfloat16)] * 2
    return simple_call(
        kernel, where, [in_hbm(), in_hbm()], shape, key_rows, value_rows,
        scratch=[pltpu.SemaphoreType.DMA((4 * MINE,))],
    )


def local_kv_call(where, own_kv, got_kv):
    def kernel(where_ref, own, got, *outs):
        for h, out in enumerate(outs):
            out[0] = own[h]
            out[1] = got[h]

    shape = [jax.ShapeDtypeStruct((2,) + own_kv.shape[1:], jnp.bfloat16) for _ in range(MINE)]
    return simple_call(kernel, where, [in_vmem()] * 2, shape, own_kv, got_kv)


def split_qg_call(where, query_rows, out_grad, loss_mask, after):
    rows = query_rows.shape[1]
    heads = MINE * GROUP
    width = heads * HD

    def kernel(where_ref, q_ref, g_ref, mask_ref, after_ref, give, own, token, g_s, sems):
        parity = where_ref[0] & 1
        pieces = []
        for i, (base, out) in enumerate(((1 - parity, give), (parity, own))):
            columns = pl.ds(pl.multiple_of(base * width, width), width)
            g_copy = pltpu.make_async_copy(g_ref.at[0, :, columns], g_s.at[i], sems.at[i, 0])
            g_copy.start()
            q_copies = []
            for h in range(heads):
                one = pl.ds(pl.multiple_of(base * width + h * HD, HD), HD)
                q_copies.append(
                    pltpu.make_async_copy(q_ref.at[0, :, one], out.at[0, h], sems.at[i, 1 + h])
                )
                q_copies[-1].start()
            pieces.append((g_copy, q_copies, out))
        keep_rows = mask_column(mask_ref)
        local = jnp.sum(mask_ref[...].astype(jnp.float32), axis=1, keepdims=True)
        token[...] = jnp.broadcast_to(local, token.shape)
        for i, (g_copy, q_copies, out) in enumerate(pieces):
            g_copy.wait()
            for h in range(heads):
                columns = slice(h * HD, (h + 1) * HD)
                out[1, h] = (g_s[i, :, columns].astype(jnp.float32) * keep_rows).astype(
                    jnp.bfloat16
                )
            for copy in q_copies:
                copy.wait()

    shape = [
        jax.ShapeDtypeStruct((2, heads, rows, HD), jnp.bfloat16),
        jax.ShapeDtypeStruct((2, heads, rows, HD), jnp.bfloat16),
        jax.ShapeDtypeStruct((8, HD), jnp.float32),
    ]
    return simple_call(
        kernel, where, [in_hbm(), in_hbm(), in_vmem(), pl.BlockSpec(memory_space=pl.ANY)], shape,
        query_rows, out_grad, loss_mask, after,
        scratch=[pltpu.VMEM((2, rows, width), jnp.bfloat16), pltpu.SemaphoreType.DMA((2, 1 + heads))],
    )


def total_call(where, numerator, part, count):
    rows = part[0].shape[2]

    def kernel(where_ref, d0, r1, r2, count_ref, own, give):
        scale = numerator / count_ref[0:1, :]
        for kv, factor in enumerate((scale * HD ** (-0.5), scale)):
            for p, out in enumerate((own, give)):
                out[kv] = (
                    (d0[p, kv] + r1[p, kv].astype(jnp.float32) + r2[p, kv].astype(jnp.float32))
                    * factor
                ).astype(jnp.bfloat16)

    shape = [jax.ShapeDtypeStruct((2, rows, HD), jnp.bfloat16)] * 2
    return simple_call(kernel, where, [in_vmem() for _ in range(4)], shape, *part, count)


def finish_kv_call(where, own, got):
    rows = own[0].shape[1]
    width = MINE * HD

    def kernel(where_ref, *refs):
        parity = where_ref[0] & 1
        outs = refs[2 * MINE :]
        for base, parts in ((parity, refs[:MINE]), (1 - parity, refs[MINE : 2 * MINE])):
            for h, part in enumerate(parts):
                at = pl.ds(pl.multiple_of(base * width + h * HD, HD), HD)
                for kv, out in enumerate(outs):
                    out[0, :, at] = part[kv]

    shape = [jax.ShapeDtypeStruct((1, rows, 2 * width), jnp.bfloat16)] * 2
    args = list(own) + list(got)
    return simple_call(kernel, where, [in_vmem() for _ in args], shape, *args)


def finish_q_call(where, numerator, own, got, count):
    rows = own[0].shape[0]
    wide = GROUP * HD
    width = MINE * wide

    def kernel(where_ref, *refs):
        own_refs = refs[:MINE]
        got_refs = refs[MINE : 2 * MINE]
        count_ref, out, token = refs[2 * MINE :]
        token[...] = count_ref[...]
        scale = numerator / count_ref[0:1, :] * HD ** (-0.5)
        parity = where_ref[0] & 1
        for base, parts in ((parity * width, own_refs), ((1 - parity) * width, got_refs)):
            for h, part in enumerate(parts):
                for j in range(GROUP):
                    at = pl.multiple_of(base + h * wide + j * HD, HD)
                    value = part[:, j * HD : (j + 1) * HD].astype(jnp.float32) * scale
                    out[0, :, pl.ds(at, HD)] = value.astype(out.dtype)

    shape = [
        jax.ShapeDtypeStruct((1, rows, 2 * width), jnp.bfloat16),
        jax.ShapeDtypeStruct(count.shape, count.dtype),
    ]
    args = list(own) + list(got) + [count]
    return simple_call(kernel, where, [in_vmem() for _ in args], shape, *args)


def grads_kernel(
    where_ref, lengths_ref, own_qg, got_qg, kv0, kv1, kv2,
    own_dq, sib_dq, out0, out1, out2,
    k_s, v_s, kt_s, bias_s, e_s, dp_s, mb_s, m_s, top_s, l_s, w_s, dqt_s, dk_s, dv_s,
):
    rows = own_qg.shape[2]
    my_index = where_ref[0]
    doc_count = lengths_ref.shape[1]
    for d, kv in enumerate((kv0, kv1, kv2)):
        for p in range(2):
            k_s[2 * d + p] = kv[p, 0]
            v_s[2 * d + p] = kv[p, 1]
            kt_s[2 * d + p] = kv[p, 0].T
    dk_s[...] = jnp.zeros_like(dk_s)
    dv_s[...] = jnp.zeros_like(dv_s)

    def per_q(qb, qg, dq):
        q_s, g_s = qg.at[0], qg.at[1]
        q_start = (my_index ^ qb) * rows

        def doc_step(j, state):
            bound, first, last, lo = state
            bound = bound + lengths_ref[0, j]
            first = jnp.where(bound <= q_start, bound, first)
            last = jnp.where(bound <= q_start + rows - 1, bound, last)
            t_pos = q_start + lax.broadcasted_iota(jnp.int32, (1, rows), 1)
            lo = jnp.where(bound <= t_pos, bound, lo)
            return bound, first, last, lo

        zero = jnp.int32(0)
        _, first, last, lo = lax.fori_loop(
            0, doc_count, doc_step, (zero, zero, zero, jnp.zeros((1, rows), jnp.int32))
        )
        t_pos = q_start + lax.broadcasted_iota(jnp.int32, (1, rows), 1)
        dqt_s[...] = jnp.zeros_like(dqt_s)

        def locate(j):
            kb = jnp.where(j < 2, j ^ qb, j)
            k_start = ((my_index ^ (kb & 1)) - (kb // 2) * 2) * rows
            live = (k_start >= 0) & (k_start <= q_start) & (k_start + rows > first)
            return kb, k_start, live

        def is_full(k_start):
            return (k_start < q_start) & (k_start >= last)

        def mask_step(j, _):
            kb, k_start, live = locate(j)

            @pl.when(live & jnp.logical_not(is_full(k_start)))
            def _():
                u_pos = k_start + lax.broadcasted_iota(jnp.int32, (rows, rows), 0)
                bias_s[kb] = jnp.where((u_pos >= lo) & (u_pos <= t_pos), 0.0, -jnp.inf)

            return 0

        lax.fori_loop(0, BLOCKS, mask_step, 0)

        def block(kb, masked, fixed):
            k = k_s[kb]
            v = v_s[kb]
            for h in range(GROUP):
                s = nt(k, q_s[h])
                if masked:
                    s = s + bias_s[kb]
                dp = nt(v, g_s[h])
                top = jnp.max(s, axis=0, keepdims=True)
                if fixed:
                    m_new = m_s[h]
                    top_s[h] = jnp.maximum(top_s[h], top)
                    old_l, old_w = l_s[h], w_s[h]
                else:
                    m_new = jnp.maximum(m_s[h], top)
                    keep = jnp.exp2((m_s[h] - m_new) * EXP2_SCALE)
                    old_l, old_w = l_s[h] * keep, w_s[h] * keep
                    m_s[h] = m_new
                    top_s[h] = m_new
                e = jnp.exp2((s - m_new) * EXP2_SCALE)
                l_s[h] = old_l + jnp.sum(e, axis=0, keepdims=True)
                w_s[h] = old_w + jnp.sum(e * dp, axis=0, keepdims=True)
                mb_s[kb * GROUP + h] = m_new
                e_s[kb * GROUP + h] = e
                dp_s[kb * GROUP + h] = dp

        def steps(fixed):
            def step(j, _):
                kb, k_start, live = locate(j)

                @pl.when(live & is_full(k_start))
                def _():
                    block(kb, False, fixed)

                @pl.when(live & jnp.logical_not(is_full(k_start)))
                def _():
                    block(kb, True, fixed)

                return 0

            return step

        def begin():
            m_s[...] = jnp.full_like(m_s, -jnp.inf)
            l_s[...] = jnp.zeros_like(l_s)
            w_s[...] = jnp.zeros_like(w_s)

        begin()
        block(qb, True, False)
        lax.fori_loop(1, BLOCKS, steps(True), 0)
        excess = jnp.max((top_s[...] - m_s[...]) * EXP2_SCALE)

        @pl.when(jnp.logical_not(excess <= MOST_EXCESS))
        def _():
            begin()
            lax.fori_loop(0, BLOCKS, steps(False), 0)

        def phase_b(j, _):
            kb, _, live = locate(j)

            @pl.when(live)
            def _():
                p_all = []
                ds_all = []
                for h in range(GROUP):
                    inverse = 1.0 / l_s[h]
                    grad_dot = w_s[h] * inverse
                    alpha = jnp.exp2((mb_s[kb * GROUP + h] - m_s[h]) * EXP2_SCALE) * inverse
                    p = e_s[kb * GROUP + h] * alpha
                    ds_all.append((p * (dp_s[kb * GROUP + h] - grad_dot)).astype(jnp.bfloat16))
                    p_all.append(p.astype(jnp.bfloat16))
                ds = jnp.concatenate(ds_all, 1)
                dv_s[kb] += nn(jnp.concatenate(p_all, 1), g_s[...].reshape(GROUP * rows, HD))
                dk_s[kb] += nn(ds, q_s[...].reshape(GROUP * rows, HD))
                dqt_s[...] += nn(kt_s[kb], ds)

            return 0

        lax.fori_loop(0, BLOCKS, phase_b, 0)

        for h in range(GROUP):
            dq[:, h * HD : (h + 1) * HD] = dqt_s[:, h * rows : (h + 1) * rows].T.astype(dq.dtype)

    per_q(0, own_qg, own_dq)
    per_q(1, got_qg, sib_dq)
    for d, out in enumerate((out0, out1, out2)):
        for p in range(2):
            out[p, 0] = dk_s[2 * d + p].astype(out.dtype)
            out[p, 1] = dv_s[2 * d + p].astype(out.dtype)


def grads_call(head, where, lengths, own_qg, got_qg, kv0, kv1, kv2):
    rows = own_qg.shape[2]
    wide = GROUP * HD
    half = pl.BlockSpec((2, GROUP, rows, HD), lambda i, w: (0, head, 0, 0))
    f32 = jnp.float32
    bf16 = jnp.bfloat16
    tiles = BLOCKS * GROUP
    tile_work = 2 * rows * rows * HD
    return pl.pallas_call(
        grads_kernel,
        grid_spec=pltpu.PrefetchScalarGridSpec(
            num_scalar_prefetch=1,
            grid=(1,),
            in_specs=[
                pl.BlockSpec(memory_space=pltpu.SMEM),
                half, half, in_vmem(), in_vmem(), in_vmem(),
            ],
            out_specs=[in_vmem() for _ in range(5)],
            scratch_shapes=[
                pltpu.VMEM((BLOCKS, rows, HD), bf16),
                pltpu.VMEM((BLOCKS, rows, HD), bf16),
                pltpu.VMEM((BLOCKS, HD, rows), bf16),
                pltpu.VMEM((BLOCKS, rows, rows), f32),
                pltpu.VMEM((tiles, rows, rows), f32),
                pltpu.VMEM((tiles, rows, rows), f32),
                pltpu.VMEM((tiles, 1, rows), f32),
                pltpu.VMEM((GROUP, 1, rows), f32),
                pltpu.VMEM((GROUP, 1, rows), f32),
                pltpu.VMEM((GROUP, 1, rows), f32),
                pltpu.VMEM((GROUP, 1, rows), f32),
                pltpu.VMEM((HD, GROUP * rows), f32),
                pltpu.VMEM((BLOCKS, rows, HD), f32),
                pltpu.VMEM((BLOCKS, rows, HD), f32),
            ],
        ),
        out_shape=[
            jax.ShapeDtypeStruct((rows, wide), bf16),
            jax.ShapeDtypeStruct((rows, wide), bf16),
            jax.ShapeDtypeStruct((2, 2, rows, HD), f32),
            jax.ShapeDtypeStruct((2, 2, rows, HD), bf16),
            jax.ShapeDtypeStruct((2, 2, rows, HD), bf16),
        ],
        compiler_params=pltpu.CompilerParams(vmem_limit_bytes=26 * 1024 * 1024),
        name="grads",
        cost_estimate=pl.CostEstimate(
            flops=5 * 6 * GROUP * tile_work, transcendentals=6 * GROUP * rows * rows,
            bytes_accessed=6 * 1024 * 1024,
        ),
    )(where, lengths, own_qg, got_qg, kv0, kv1, kv2)


def work(query_rows, key_rows, value_rows, out_grad, lengths, loss_mask):
    rows = query_rows.shape[1]
    numerator = float(lax.axis_size("dp") * rows * lax.axis_size("ctx"))
    where = lax.axis_index("ctx").astype(jnp.int32).reshape(1)

    query_rows, key_rows, value_rows, out_grad = (
        pltpu.with_memory_space_constraint(x, pltpu.HBM)
        for x in (query_rows, key_rows, value_rows, out_grad)
    )
    give_kv, own_kv = split_kv_call(where, key_rows, value_rows)
    got_kv = swapped(give_kv, 1)
    give_qg, own_qg, token = split_qg_call(where, query_rows, out_grad, loss_mask, give_kv)
    got_qg = swapped(give_qg, 1)
    local = local_kv_call(where, own_kv, got_kv)
    near = []
    far = []
    for kv in local:
        near.append(shifted(kv, 2))
        far.append(shifted(kv, 4))

    own_dq = []
    got_dq = []
    parts = []
    for h in range(MINE):
        dq_o, dq_s, d0, d1, d2 = grads_call(
            h, where, lengths, own_qg, got_qg, local[h], near[h], far[h]
        )
        own_dq.append(dq_o)
        r1 = shifted(d1, -2)
        r2 = shifted(d2, -4)
        parts.append((d0, r1, r2))
        got_dq.append(swapped(dq_s, 1))
    count = everywhere_sum(token)
    query_grad, count = finish_q_call(where, numerator, own_dq, got_dq, count)
    own_totals = []
    got_totals = []
    for part in parts:
        own_total, give_total = total_call(where, numerator, part, count)
        own_totals.append(own_total)
        got_totals.append(swapped(give_total, 1))
    key_grad, value_grad = finish_kv_call(where, own_totals, got_totals)
    return query_grad, key_grad, value_grad


def solution(mesh):
    placed = (
        P("dp", "ctx", None),
        P("dp", "ctx", None),
        P("dp", "ctx", None),
        P("dp", "ctx", None),
        P("dp", None),
        P("dp", "ctx"),
    )
    return jax.shard_map(
        work,
        mesh=mesh,
        in_specs=placed,
        out_specs=(P("dp", "ctx", None), P("dp", "ctx", None), P("dp", "ctx", None)),
        check_vma=False,
    )
```
